32 devices in a mesh: sec: 8 (over z, x), blk: 4 (over y, core).
Axes of the slice: x: 2, y: 2, z: 4, core: 2. Of those that a mesh axis runs over, the one named last changes fastest.
Arguments:
- features: bfloat16 [8, 52, 8192], P('sec', None, 'blk'), may hold values from -6 to 6
- programs: bfloat16 [8, 32, 8192], P('sec', None, 'blk'), may hold values from -6 to 6
- column_pot: bfloat16 [8, 8192], P('sec', 'blk'), may hold values from -12 to 12
- tile_pairs: int32 [2, 8, 112], P(None, 'sec', 'blk'), may hold values from 0 to 15, as said below
- pair_counts: int32 [8, 4], P('sec', 'blk'), may hold values from 0 to 28, as said below
Outputs:
- smoothed: bfloat16 [8, 32, 8192], P('sec', None, 'blk')
- row_potential: float32 [8, 8192], P('sec', 'blk')
- column_potential: float32 [8, 8192], P('sec', 'blk')
The draws below stay inside these ranges and needn't reach their ends.
Inputs may be any that keep to these rules, and one draw needn't show every extreme that they name: `tile_pairs`: entry [0, s, b * 28 + k] is a row tile of block b of section s counted within the block (0 to 3); entry [1, s, b * 28 + k] is a tile of section s + 1 (0 to 15). Only slots k < pair_counts[s, b] are active; slots from there on hold in-range entries that do not count. The active pairs of one block are distinct; in every section but the last, every row tile of every block is in an active pair, and every tile of section s + 1 is in an active pair of section s. `pair_counts`: 0 in the last section; in every other section from 4 to 28, and one block of every such section holds exactly 28.
All inputs are finite; a program needn't handle non-finite values.
Results may differ from the reference program's by a relative error of at most 0.0034.
Values may be sent and summed in bfloat16 or wider, within the bound.
A program may use at most 64 MiB of HBM per device.

```python
import jax
import jax.numpy as jnp
from jax import lax

FEAT = 52
PROGS = 32
TILE = 512
TILES_BLK = 4
SECTIONS = 8
TILES_SEC = 16
CELLS = 8192
MAXP = 28
SLOTS = 112
N_BLK = 4


def pair_plan(key):
    dense = jax.random.randint(jax.random.fold_in(key, 11), (SECTIONS,), 0, N_BLK)
    lighter = jax.random.randint(jax.random.fold_in(key, 12), (SECTIONS, N_BLK), TILES_BLK, TILES_BLK + TILES_BLK // 2 + 1)
    block_ids = jnp.arange(N_BLK, dtype=jnp.int32)
    section_ids = jnp.arange(SECTIONS, dtype=jnp.int32)
    counts = jnp.where(block_ids[None, :] == dense[:, None], MAXP, lighter)
    counts = jnp.where(section_ids[:, None] == SECTIONS - 1, 0, counts).astype(jnp.int32)
    shift_keys = jax.random.split(jax.random.fold_in(key, 13), SECTIONS * N_BLK)
    offsets = jax.vmap(lambda one_key: jax.random.permutation(one_key, TILES_SEC - 1) + 1)(shift_keys)
    order_keys = jax.random.split(jax.random.fold_in(key, 14), SECTIONS * N_BLK)
    row_orders = jax.vmap(lambda one_key: jax.random.permutation(one_key, TILES_BLK))(order_keys)
    slot_ids = jnp.arange(MAXP, dtype=jnp.int32)
    layer_ids = slot_ids // TILES_BLK
    within = slot_ids % TILES_BLK
    local_rows = row_orders[:, within]
    shift_table = jnp.concatenate([jnp.zeros((SECTIONS * N_BLK, 1), jnp.int32), offsets.astype(jnp.int32)], axis=1)
    shifts = shift_table[:, layer_ids]
    block_of = (jnp.arange(SECTIONS * N_BLK, dtype=jnp.int32) % N_BLK)[:, None]
    col_tiles = (block_of * TILES_BLK + local_rows + shifts) % TILES_SEC
    tiles = jnp.stack([local_rows, col_tiles]).reshape(2, SECTIONS, N_BLK * MAXP)
    return (tiles.astype(jnp.int32), counts)


def draw_tile_pairs(key, part):
    return pair_plan(key)[0]


def draw_pair_counts(key, part):
    return pair_plan(key)[1]


def draw_column_pot(key, part):
    values = 0.5 * jnp.clip(jax.random.normal(jax.random.fold_in(key, 23), (SECTIONS, CELLS), jnp.float32), -6.0, 6.0)
    return values.astype(jnp.bfloat16)


def block_levels(own_key, dims, cuts, least, top_value):
    level = 1.0
    for position, blocks in cuts:
        heights = jax.random.uniform(jax.random.fold_in(jax.random.fold_in(own_key, 6), position), (blocks,), jnp.float32, least / len(cuts), top_value / len(cuts))
        level = level * jnp.repeat(jnp.exp(heights), dims[position] // blocks).reshape((-1,) + (1,) * (len(dims) - 1 - position))
    return level


def gaussian(rng, shape, width, bound, pieces=(), kind=jnp.bfloat16):
    gain = block_levels(rng, shape, pieces, -0.22, 0.18) if pieces else 1.0
    drawn = jax.random.normal(rng, shape, jnp.float32) * width * gain
    return jnp.minimum(jnp.maximum(drawn, -bound), bound).astype(kind)


def setup_inputs(seed: int = 0) -> dict:
    keys = jax.random.split(jax.random.key(seed), 6)
    features = gaussian(keys[0], (SECTIONS, FEAT, CELLS), 1.0, 6.0, ((0, 8), (2, 4)))
    programs = gaussian(keys[1], (SECTIONS, PROGS, CELLS), 1.0, 6.0, ((0, 8), (2, 4)))
    column_pot = draw_column_pot(jax.random.fold_in(keys[5], 71), 0)
    tile_pairs = draw_tile_pairs(jax.random.fold_in(keys[5], 71), 0)
    pair_counts = draw_pair_counts(jax.random.fold_in(keys[5], 71), 0)
    return {"features": features, "programs": programs, "column_pot": column_pot, "tile_pairs": tile_pairs, "pair_counts": pair_counts}


EPSILON = 0.05
NEG_FILL = -1.0e30


def merge_lse(first_lse, second_lse):
    highest = jnp.maximum(first_lse[0], second_lse[0])
    return (highest, first_lse[1] * jnp.exp(first_lse[0] - highest) + second_lse[1] * jnp.exp(second_lse[0] - highest))


def tile_cost(row_x, row_sq, col_x, col_sq, row_tile, col_tile):
    row_block = lax.dynamic_slice_in_dim(row_x, row_tile * TILE, TILE, 1)
    col_block = lax.dynamic_slice_in_dim(col_x, col_tile * TILE, TILE, 1)
    inner = lax.dot_general(row_block, col_block, (((0,), (0,)), ((), ())), preferred_element_type=jnp.float32)
    row_part = lax.dynamic_slice_in_dim(row_sq, row_tile * TILE, TILE, 0)
    col_part = lax.dynamic_slice_in_dim(col_sq, col_tile * TILE, TILE, 0)
    return (row_part[:, None] + col_part[None, :] - 2.0 * inner) / FEAT


def fold_lse(carry_lse, scores, offset, reduce_axis, usable):
    tile_max = jnp.max(scores, axis=reduce_axis)
    tile_sum = jnp.sum(jnp.exp(scores - jnp.expand_dims(tile_max, reduce_axis)), axis=reduce_axis)
    tile_max = jnp.where(usable, tile_max, NEG_FILL)
    tile_sum = jnp.where(usable, tile_sum, 0.0)
    old_max = lax.dynamic_slice_in_dim(carry_lse[0], offset, TILE, 0)
    old_sum = lax.dynamic_slice_in_dim(carry_lse[1], offset, TILE, 0)
    new_max, new_sum = merge_lse((old_max, old_sum), (tile_max, tile_sum))
    return (lax.dynamic_update_slice_in_dim(carry_lse[0], new_max, offset, 0), lax.dynamic_update_slice_in_dim(carry_lse[1], new_sum, offset, 0))


def one_plan(row_x, col_x, row_ext, col_ext, col_pot, row_tiles, col_tiles, usable):
    row_sq = jnp.sum(jnp.square(row_x.astype(jnp.float32)), axis=0)
    col_sq = jnp.sum(jnp.square(col_x.astype(jnp.float32)), axis=0)
    pot_in = col_pot.astype(jnp.float32)
    empty = (jnp.full((CELLS,), NEG_FILL, jnp.float32), jnp.zeros((CELLS,), jnp.float32))

    def row_pass(carry_lse, item):
        row_tile, col_tile, active = item
        cost = tile_cost(row_x, row_sq, col_x, col_sq, row_tile, col_tile)
        column = lax.dynamic_slice_in_dim(pot_in, col_tile * TILE, TILE, 0)
        scores = (column[None, :] - cost) / EPSILON
        return fold_lse(carry_lse, scores, row_tile * TILE, 1, active), 0

    row_lse = lax.scan(row_pass, empty, (row_tiles, col_tiles, usable))[0]
    row_pot = -EPSILON * (row_lse[0] + jnp.log(row_lse[1]))

    def col_pass(carry_lse, item):
        row_tile, col_tile, active = item
        cost = tile_cost(row_x, row_sq, col_x, col_sq, row_tile, col_tile)
        rows_here = lax.dynamic_slice_in_dim(row_pot, row_tile * TILE, TILE, 0)
        scores = (rows_here[:, None] - cost) / EPSILON
        return fold_lse(carry_lse, scores, col_tile * TILE, 0, active), 0

    col_lse = lax.scan(col_pass, empty, (row_tiles, col_tiles, usable))[0]
    col_new = -EPSILON * (col_lse[0] + jnp.log(col_lse[1]))
    zero_num = jnp.zeros((PROGS + 1, CELLS), jnp.float32)

    def plan_pass(sums, item):
        row_tile, col_tile, active = item
        row_num, col_num = sums
        cost = tile_cost(row_x, row_sq, col_x, col_sq, row_tile, col_tile)
        rows_here = lax.dynamic_slice_in_dim(row_pot, row_tile * TILE, TILE, 0)
        cols_here = lax.dynamic_slice_in_dim(col_new, col_tile * TILE, TILE, 0)
        plan = jnp.exp((rows_here[:, None] + cols_here[None, :] - cost) / EPSILON)
        plan = jnp.where(active, plan, 0.0).astype(jnp.bfloat16)
        col_prog = lax.dynamic_slice_in_dim(col_ext, col_tile * TILE, TILE, 1)
        row_prog = lax.dynamic_slice_in_dim(row_ext, row_tile * TILE, TILE, 1)
        to_rows = lax.dot_general(col_prog, plan, (((1,), (1,)), ((), ())), preferred_element_type=jnp.float32)
        to_cols = lax.dot_general(row_prog, plan, (((1,), (0,)), ((), ())), preferred_element_type=jnp.float32)
        old_rows = lax.dynamic_slice_in_dim(row_num, row_tile * TILE, TILE, 1)
        old_cols = lax.dynamic_slice_in_dim(col_num, col_tile * TILE, TILE, 1)
        row_num = lax.dynamic_update_slice_in_dim(row_num, old_rows + to_rows, row_tile * TILE, 1)
        col_num = lax.dynamic_update_slice_in_dim(col_num, old_cols + to_cols, col_tile * TILE, 1)
        return (row_num, col_num), 0

    row_num, col_num = lax.scan(plan_pass, (zero_num, zero_num), (row_tiles, col_tiles, usable))[0]
    return row_pot, col_new, row_num, col_num


def run_plan(packed):
    return one_plan(*packed)


def reference(features, programs, column_pot, tile_pairs, pair_counts):
    ones_row = jnp.ones((SECTIONS, 1, CELLS), jnp.bfloat16)
    extended = jnp.concatenate([programs, ones_row], axis=1)
    slot_ids = jnp.arange(SLOTS, dtype=jnp.int32)
    owners = slot_ids // MAXP
    row_tiles = (tile_pairs[0] + owners[None, :] * TILES_BLK).astype(jnp.int32)
    col_tiles = tile_pairs[1].astype(jnp.int32)
    usable = (slot_ids % MAXP)[None, :] < jnp.repeat(pair_counts, MAXP, axis=1)
    packed = (features[:-1], features[1:], extended[:-1], extended[1:], column_pot[:-1], row_tiles[:-1], col_tiles[:-1], usable[:-1])
    row_pot, col_pot, row_num, col_num = lax.map(run_plan, packed)
    zero_row = jnp.zeros((1, CELLS), jnp.float32)
    zero_num = jnp.zeros((1, PROGS + 1, CELLS), jnp.float32)
    row_potential = jnp.concatenate([row_pot, zero_row], axis=0)
    column_potential = jnp.concatenate([col_pot, zero_row], axis=0)
    totals = jnp.concatenate([row_num, zero_num], axis=0) + jnp.concatenate([zero_num, col_num], axis=0)
    smoothed = (totals[:, :PROGS] / totals[:, PROGS:]).astype(jnp.bfloat16)
    return smoothed, row_potential, column_potential
```

```python
import functools
import math

import jax
import jax.numpy as jnp
from jax import lax
from jax.experimental import pallas as pl
from jax.experimental.pallas import tpu as pltpu
from jax.sharding import PartitionSpec as P

TILE = 512
EPSILON = 0.05
LOG2E = math.log2(math.e)
LN2 = math.log(2.0)
NEG = -1e30
UNROLL = 4
HALF = 64
EXT = 48


def split3(value):
    hi = value.astype(jnp.bfloat16).astype(jnp.float32)
    rest = value - hi
    mid = rest.astype(jnp.bfloat16).astype(jnp.float32)
    return hi, mid, rest - mid


def rows_of(pieces, width):
    index = lax.broadcasted_iota(jnp.int32, (8, width), 0)
    block = jnp.zeros((8, width), jnp.float32)
    for place, piece in enumerate(pieces):
        block = jnp.where(index == place, piece, block)
    return block


def sum_squares(cells):
    return jnp.sum(cells * cells, axis=0, keepdims=True)


def own_records(own_ref, xrec, feat, slice_of, tiles_blk, tiles, bias_of):
    width = TILE // (tiles // tiles_blk)
    gain = 2.0 * LOG2E / (feat * EPSILON)
    xrec[...] = jnp.zeros_like(xrec)

    def one(tile, carry):
        start = pl.multiple_of((tile % tiles_blk) * TILE + slice_of * width, width)
        cells = own_ref[tile // tiles_blk, 0:feat, pl.ds(start, width)].astype(jnp.float32)
        scaled = cells * gain
        high = scaled.astype(jnp.bfloat16)
        xrec[tile, 0:feat, :] = high
        xrec[tile, HALF : HALF + feat, :] = (scaled - high.astype(jnp.float32)).astype(jnp.bfloat16)
        bias = split3(bias_of(tile, cells))
        ones = jnp.ones((1, width), jnp.float32)
        aux = rows_of((ones, ones, ones) + bias, width)
        xrec[tile, HALF - 8 : HALF, :] = aux.astype(jnp.bfloat16)
        return carry

    lax.fori_loop(0, tiles, one, 0)


def other_records(other_ref, yrec, build, feat, tiles_blk, tiles, bias_of):
    build[...] = jnp.zeros_like(build)
    ones = jnp.ones((1, TILE), jnp.float32)

    def one(tile, carry):
        start = pl.multiple_of((tile % tiles_blk) * TILE, TILE)
        cells = other_ref[tile // tiles_blk, 0:feat, pl.ds(start, TILE)].astype(jnp.float32)
        build[0:feat, :] = cells
        build[HALF : HALF + feat, :] = cells
        bias = split3(bias_of(tile, start, cells))
        build[HALF - 8 : HALF, :] = rows_of(bias + (ones, ones, ones), TILE)
        yrec[pl.ds(pl.multiple_of(tile * TILE, TILE), TILE), :] = build[...].T.astype(jnp.bfloat16)
        return carry

    lax.fori_loop(0, tiles, one, 0)
    lane = lax.broadcasted_iota(jnp.int32, (TILE, 2 * HALF), 1)
    yrec[tiles * TILE : (tiles + 1) * TILE, :] = jnp.where(lane == HALF - 8, NEG, 0.0).astype(
        jnp.bfloat16
    )


def ext_records(prog_ref, ext, progs, tiles_blk, tiles):
    index = lax.broadcasted_iota(jnp.int32, (EXT - progs, TILE), 0)
    tail = jnp.where(index == 0, 1.0, 0.0).astype(jnp.bfloat16)

    def one(tile, carry):
        start = pl.multiple_of((tile % tiles_blk) * TILE, TILE)
        ext[tile, 0:progs, :] = prog_ref[tile // tiles_blk, :, pl.ds(start, TILE)]
        ext[tile, progs:EXT, :] = tail
        return carry

    lax.fori_loop(0, tiles, one, 0)
    ext[tiles] = jnp.zeros((EXT, TILE), jnp.bfloat16)


def listed_pairs(lists_ref, mine, other, most, blocks, tiles_blk, tiles, own_first):
    def of_block(block, place):
        def one(slot, at):
            row = lists_ref[block, slot] + block * tiles_blk
            col = lists_ref[block, most + slot]
            mine[at] = row if own_first else col
            other[at] = col if own_first else row
            return at + 1

        return lax.fori_loop(0, lists_ref[block, 2 * most], one, place)

    total = lax.fori_loop(0, blocks, of_block, 0)
    last = mine[jnp.maximum(total - 1, 0)]
    for extra in range(UNROLL - 1):
        mine[total + extra] = last
        other[total + extra] = tiles
    return (total + UNROLL - 1) // UNROLL


def scores_of(yrec, xrec, mine, other):
    rows = yrec[pl.ds(pl.multiple_of(other * TILE, TILE), TILE), :]
    return jnp.dot(rows, xrec[mine], preferred_element_type=jnp.float32)


def spread(parts_ref, tile, blocks):
    return jnp.concatenate([parts_ref[block, pl.ds(tile, 1), :] for block in range(blocks)], axis=1)


def row_kernel(dims, lists_ref, own_ref, next_ref, pot_ref, rp_ref, xrec, yrec, build, high, total, mine, other):
    feat, blocks, tiles_blk, most = dims
    tiles = blocks * tiles_blk
    to_score = LOG2E / EPSILON
    groups = listed_pairs(lists_ref, mine, other, most, blocks, tiles_blk, tiles, True)
    own_records(
        own_ref, xrec, feat, lax.axis_index("blk"), tiles_blk, tiles,
        lambda tile, cells: jnp.zeros((1, cells.shape[1]), jnp.float32),
    )

    def bias(tile, start, cells):
        pot = pot_ref[tile // tiles_blk, :, pl.ds(start, TILE)].astype(jnp.float32)
        return (pot - sum_squares(cells) / feat) * to_score

    other_records(next_ref, yrec, build, feat, tiles_blk, tiles, bias)
    high[...] = jnp.full_like(high, NEG)
    total[...] = jnp.zeros_like(total)

    def group(index, carry):
        for step in range(UNROLL):
            at = index * UNROLL + step
            row = mine[at]
            scores = scores_of(yrec, xrec, row, other[at])
            old = high[row]
            new = jnp.maximum(old, jnp.max(scores, axis=0, keepdims=True))
            part = jnp.sum(jnp.exp2(scores - new), axis=0, keepdims=True)
            total[row] = total[row] * jnp.exp2(old - new) + part
            high[row] = new
        return carry

    lax.fori_loop(0, groups, group, 0)
    at_end = lax.axis_index("sec") == lax.axis_size("sec") - 1
    width = TILE // blocks
    for tile in range(tiles):
        start = pl.multiple_of((tile % tiles_blk) * TILE + lax.axis_index("blk") * width, width)
        cells = own_ref[tile // tiles_blk, 0:feat, pl.ds(start, width)].astype(jnp.float32)
        score = high[tile] + jnp.log2(total[tile]) - sum_squares(cells) * (to_score / feat)
        rp_ref[tile : tile + 1, :] = jnp.where(at_end, 0.0, score * (-EPSILON * LN2))


def col_kernel(dims, lists_ref, own_ref, prev_ref, rp_ref, prog_ref, cp_ref, back_ref,
               xrec, yrec, build, ext, high, total, acc, mine, other):
    feat, blocks, tiles_blk, most = dims
    tiles = blocks * tiles_blk
    to_score = LOG2E / EPSILON
    progs = prog_ref.shape[1]
    groups = listed_pairs(lists_ref, mine, other, most, blocks, tiles_blk, tiles, False)
    own_records(
        own_ref, xrec, feat, lax.axis_index("blk"), tiles_blk, tiles,
        lambda tile, cells: jnp.zeros((1, cells.shape[1]), jnp.float32),
    )

    def bias(tile, start, cells):
        return (spread(rp_ref, tile, blocks) - sum_squares(cells) / feat) * to_score

    other_records(prev_ref, yrec, build, feat, tiles_blk, tiles, bias)
    ext_records(prog_ref, ext, progs, tiles_blk, tiles)
    high[...] = jnp.full_like(high, NEG)
    total[...] = jnp.zeros_like(total)
    acc[...] = jnp.zeros_like(acc)

    def group(index, carry):
        for step in range(UNROLL):
            at = index * UNROLL + step
            col, row = mine[at], other[at]
            scores = scores_of(yrec, xrec, col, row)
            old = high[col]
            new = jnp.maximum(old, jnp.max(scores, axis=0, keepdims=True))
            weight = jnp.exp2(scores - new)
            part = jnp.sum(weight, axis=0, keepdims=True)
            shrink = jnp.exp2(old - new)
            sums = jnp.dot(ext[row], weight.astype(jnp.bfloat16), preferred_element_type=jnp.float32)
            acc[col] = acc[col] * shrink + sums
            total[col] = total[col] * shrink + part
            high[col] = new
        return carry

    lax.fori_loop(0, groups, group, 0)
    width = TILE // blocks
    for tile in range(tiles):
        start = pl.multiple_of((tile % tiles_blk) * TILE + lax.axis_index("blk") * width, width)
        cells = own_ref[tile // tiles_blk, 0:feat, pl.ds(start, width)].astype(jnp.float32)
        filled = total[tile] > 0.0
        score = high[tile] + jnp.log2(total[tile]) - sum_squares(cells) * (to_score / feat)
        cp_ref[tile : tile + 1, :] = jnp.where(filled, score * (-EPSILON * LN2), 0.0)
        back_ref[tile] = jnp.where(filled, acc[tile] / total[tile], 0.0)


def plan_kernel(dims, lists_ref, own_ref, next_ref, rp_ref, cp_ref, prog_ref, back_ref, out_ref,
                xrec, yrec, build, ext, acc, mine, other):
    feat, blocks, tiles_blk, most = dims
    tiles = blocks * tiles_blk
    to_score = LOG2E / EPSILON
    progs = prog_ref.shape[1]
    groups = listed_pairs(lists_ref, mine, other, most, blocks, tiles_blk, tiles, True)
    own_records(
        own_ref, xrec, feat, lax.axis_index("blk"), tiles_blk, tiles,
        lambda tile, cells: (rp_ref[pl.ds(tile, 1), :] - sum_squares(cells) / feat) * to_score,
    )

    def bias(tile, start, cells):
        return (spread(cp_ref, tile, blocks) - sum_squares(cells) / feat) * to_score

    other_records(next_ref, yrec, build, feat, tiles_blk, tiles, bias)
    ext_records(prog_ref, ext, progs, tiles_blk, tiles)
    acc[...] = back_ref[...]

    def group(index, carry):
        for step in range(UNROLL):
            at = index * UNROLL + step
            row, col = mine[at], other[at]
            plan = jnp.exp2(scores_of(yrec, xrec, row, col)).astype(jnp.bfloat16)
            acc[row] = acc[row] + jnp.dot(ext[col], plan, preferred_element_type=jnp.float32)
        return carry

    lax.fori_loop(0, groups, group, 0)
    for tile in range(tiles):
        sums = acc[tile]
        out_ref[tile] = (sums[0:progs] / sums[progs : progs + 1]).astype(jnp.bfloat16)


def passed_along(value, steps):
    count = lax.axis_size("sec")
    first, last = max(0, -steps), min(count, count - steps)
    return lax.ppermute(value, "sec", [(source, source + steps) for source in range(first, last)])


def call(kernel, out_shape, operands, scratch):
    specs = [pl.BlockSpec(memory_space=pltpu.SMEM)]
    specs += [pl.BlockSpec(memory_space=pltpu.VMEM)] * (len(operands) - 1)
    outs = jax.tree.map(lambda _: pl.BlockSpec(memory_space=pltpu.VMEM), out_shape)
    return pl.pallas_call(
        kernel, out_shape=out_shape, in_specs=specs, out_specs=outs, scratch_shapes=scratch,
    )(*operands)


def body(features, programs, column_pot, tile_pairs, pair_counts):
    feat, cells_blk = features.shape[1:]
    progs = programs.shape[1]
    tiles_blk = cells_blk // TILE
    most = tile_pairs.shape[2]
    blocks = lax.axis_size("blk")
    tiles = tiles_blk * blocks
    width = TILE // blocks
    dims = (feat, blocks, tiles_blk, most)
    block = lax.axis_index("blk")

    gather = functools.partial(lax.all_gather, axis_name="blk")
    x_next, x_prev = passed_along(features[0], -1), passed_along(features[0], 1)
    lists = gather(jnp.concatenate([tile_pairs[0, 0], tile_pairs[1, 0], pair_counts[0]]))
    own = gather(features[0])
    pot = gather(column_pot)
    nexts = gather(x_next)
    prevs = gather(x_prev)
    prog_next, prog_prev = passed_along(programs[0], -1), passed_along(programs[0], 1)
    prog_next, prog_prev = gather(prog_next), gather(prog_prev)
    lists_prev = passed_along(lists, 1)

    f32, bf16 = jnp.float32, jnp.bfloat16
    xrec = pltpu.VMEM((tiles, 2 * HALF, width), bf16)
    yrec = pltpu.VMEM(((tiles + 1) * TILE, 2 * HALF), bf16)
    build = pltpu.VMEM((2 * HALF, TILE), f32)
    ext = pltpu.VMEM((tiles + 1, EXT, TILE), bf16)
    stat = pltpu.VMEM((tiles, 1, width), f32)
    acc = pltpu.VMEM((tiles, EXT, width), f32)
    index = pltpu.SMEM((blocks * most + UNROLL,), jnp.int32)
    pots = jax.ShapeDtypeStruct((tiles, width), f32)
    sums = jax.ShapeDtypeStruct((tiles, EXT, width), f32)

    row_own = call(
        functools.partial(row_kernel, dims), pots, (lists, own, nexts, pot),
        [xrec, yrec, build, stat, stat, index, index],
    )
    row_all = gather(row_own)
    row_prev = passed_along(row_all, 1)
    col_own, back = call(
        functools.partial(col_kernel, dims), (pots, sums), (lists_prev, own, prevs, row_prev, prog_prev),
        [xrec, yrec, build, ext, stat, stat, acc, index, index],
    )
    col_all = passed_along(gather(col_own), -1)
    smooth = call(
        functools.partial(plan_kernel, dims),
        jax.ShapeDtypeStruct((tiles, progs, width), bf16),
        (lists, own, nexts, row_own, col_all, prog_next, back),
        [xrec, yrec, build, ext, acc, index, index],
    )
    smooth = lax.all_to_all(smooth.reshape(blocks, tiles_blk, progs, width), "blk", 0, 0)
    smoothed = smooth.transpose(2, 1, 0, 3).reshape(1, progs, cells_blk)

    def own_part(parts):
        mine = lax.dynamic_slice_in_dim(parts, block * tiles_blk, tiles_blk, 1)
        return mine.transpose(1, 0, 2).reshape(1, cells_blk)

    return smoothed, own_part(row_all), own_part(col_all)


def solution(mesh):
    in_specs = (
        P("sec", None, "blk"),
        P("sec", None, "blk"),
        P("sec", "blk"),
        P(None, "sec", "blk"),
        P("sec", "blk"),
    )
    out_specs = (P("sec", None, "blk"), P("sec", "blk"), P("sec", "blk"))
    return jax.shard_map(body, mesh=mesh, in_specs=in_specs, out_specs=out_specs, check_vma=False)
```

```python
import functools
import math

import jax
import jax.numpy as jnp
from jax import lax
from jax.experimental import pallas as pl
from jax.experimental.pallas import tpu as pltpu
from jax.sharding import PartitionSpec as P

TILE = 512
EPSILON = 0.05
LOG2E = math.log2(math.e)
LN2 = math.log(2.0)
NEG = -1e30
UNROLL = 4
HALF = 64
EXT = 48


def split3(value):
    hi = value.astype(jnp.bfloat16).astype(jnp.float32)
    rest = value - hi
    mid = rest.astype(jnp.bfloat16).astype(jnp.float32)
    return hi, mid, rest - mid


def rows_of(pieces, width):
    index = lax.broadcasted_iota(jnp.int32, (8, width), 0)
    block = jnp.zeros((8, width), jnp.float32)
    for place, piece in enumerate(pieces):
        block = jnp.where(index == place, piece, block)
    return block


def sum_squares(cells):
    return jnp.sum(cells * cells, axis=0, keepdims=True)


def own_records(own_ref, xrec, feat, tiles_blk, tiles, bias_of):
    width = TILE // (tiles // tiles_blk)
    gain = 2.0 * LOG2E / (feat * EPSILON)
    xrec[...] = jnp.zeros_like(xrec)

    def one(tile, carry):
        cells = own_ref[tile // tiles_blk, tile % tiles_blk].astype(jnp.float32)
        scaled = cells * gain
        high = scaled.astype(jnp.bfloat16)
        xrec[tile, 0:feat, :] = high
        xrec[tile, HALF : HALF + feat, :] = (scaled - high.astype(jnp.float32)).astype(jnp.bfloat16)
        bias = split3(bias_of(tile, cells))
        ones = jnp.ones((1, width), jnp.float32)
        aux = rows_of((ones, ones, ones) + bias, width)
        xrec[tile, HALF - 8 : HALF, :] = aux.astype(jnp.bfloat16)
        return carry

    lax.fori_loop(0, tiles, one, 0)


def other_records(other_ref, yrec, build, feat, tiles_blk, tiles, bias_of):
    build[...] = jnp.zeros_like(build)
    ones = jnp.ones((1, TILE), jnp.float32)

    def one(tile, carry):
        start = pl.multiple_of((tile % tiles_blk) * TILE, TILE)
        cells = other_ref[tile // tiles_blk, 0:feat, pl.ds(start, TILE)].astype(jnp.float32)
        build[0:feat, :] = cells
        build[HALF : HALF + feat, :] = cells
        bias = split3(bias_of(tile, start, cells))
        build[HALF - 8 : HALF, :] = rows_of(bias + (ones, ones, ones), TILE)
        yrec[pl.ds(pl.multiple_of(tile * TILE, TILE), TILE), :] = build[...].T.astype(jnp.bfloat16)
        return carry

    lax.fori_loop(0, tiles, one, 0)
    lane = lax.broadcasted_iota(jnp.int32, (TILE, 2 * HALF), 1)
    yrec[tiles * TILE : (tiles + 1) * TILE, :] = jnp.where(lane == HALF - 8, NEG, 0.0).astype(
        jnp.bfloat16
    )


def ext_records(prog_ref, ext, progs, tiles_blk, tiles):
    index = lax.broadcasted_iota(jnp.int32, (EXT - progs, TILE), 0)
    tail = jnp.where(index == 0, 1.0, 0.0).astype(jnp.bfloat16)

    def one(tile, carry):
        start = pl.multiple_of((tile % tiles_blk) * TILE, TILE)
        ext[tile, 0:progs, :] = prog_ref[tile // tiles_blk, :, pl.ds(start, TILE)]
        ext[tile, progs:EXT, :] = tail
        return carry

    lax.fori_loop(0, tiles, one, 0)
    ext[tiles] = jnp.zeros((EXT, TILE), jnp.bfloat16)


def listed_pairs(lists_ref, mine, other, most, blocks, tiles_blk, tiles, own_first, used=True):
    def of_block(block, place):
        def one(slot, at):
            row = lists_ref[block, 0, slot] + block * tiles_blk
            col = lists_ref[block, 0, most + slot]
            mine[at] = row if own_first else col
            other[at] = col if own_first else row
            return at + 1

        return lax.fori_loop(0, jnp.where(used, lists_ref[block, 0, 2 * most], 0), one, place)

    total = lax.fori_loop(0, blocks, of_block, 0)
    last = mine[jnp.maximum(total - 1, 0)]
    for extra in range(UNROLL - 1):
        mine[total + extra] = last
        other[total + extra] = tiles
    return (total + UNROLL - 1) // UNROLL


def scores_of(yrec, xrec, mine, other):
    rows = yrec[pl.ds(pl.multiple_of(other * TILE, TILE), TILE), :]
    return jnp.dot(rows, xrec[mine], preferred_element_type=jnp.float32)


def spread(parts_ref, tile, blocks, tiles_blk):
    parts = [parts_ref[block, tile // tiles_blk, pl.ds(tile % tiles_blk, 1), :] for block in range(blocks)]
    return jnp.concatenate(parts, axis=1)


def near_side(forward):
    odd = lax.axis_index("sec") % 2
    return odd if forward else 1 - odd


def row_kernel(dims, lists_ref, own_ref, next_ref, pot_ref, rp_ref, xrec, yrec, build, high, total, mine, other):
    feat, blocks, tiles_blk, most = dims
    tiles = blocks * tiles_blk
    to_score = LOG2E / EPSILON
    groups = listed_pairs(lists_ref, mine, other, most, blocks, tiles_blk, tiles, True)
    own_records(
        own_ref, xrec, feat, tiles_blk, tiles,
        lambda tile, cells: jnp.zeros((1, cells.shape[1]), jnp.float32),
    )

    def bias(tile, start, cells):
        pot = pot_ref[tile // tiles_blk, :, pl.ds(start, TILE)].astype(jnp.float32)
        return (pot - sum_squares(cells) / feat) * to_score

    other_records(next_ref.at[near_side(True)], yrec, build, feat, tiles_blk, tiles, bias)
    high[...] = jnp.full_like(high, NEG)
    total[...] = jnp.zeros_like(total)

    def group(index, carry):
        for step in range(UNROLL):
            at = index * UNROLL + step
            row = mine[at]
            scores = scores_of(yrec, xrec, row, other[at])
            old = high[row]
            new = jnp.maximum(old, jnp.max(scores, axis=0, keepdims=True))
            part = jnp.sum(jnp.exp2(scores - new), axis=0, keepdims=True)
            total[row] = total[row] * jnp.exp2(old - new) + part
            high[row] = new
        return carry

    lax.fori_loop(0, groups, group, 0)
    at_end = lax.axis_index("sec") == lax.axis_size("sec") - 1
    for tile in range(tiles):
        cells = own_ref[tile // tiles_blk, tile % tiles_blk].astype(jnp.float32)
        score = high[tile] + jnp.log2(total[tile]) - sum_squares(cells) * (to_score / feat)
        rp_ref[tile // tiles_blk, tile % tiles_blk : tile % tiles_blk + 1, :] = jnp.where(at_end, 0.0, score * (-EPSILON * LN2))


def col_kernel(dims, lists_ref, own_ref, prev_ref, rp_ref, prog_ref, cp_ref, back_ref,
               xrec, yrec, build, ext, high, total, acc, mine, other):
    feat, blocks, tiles_blk, most = dims
    tiles = blocks * tiles_blk
    to_score = LOG2E / EPSILON
    progs = prog_ref.shape[2]
    used = lax.axis_index("sec") > 0
    groups = listed_pairs(
        lists_ref.at[near_side(False)], mine, other, most, blocks, tiles_blk, tiles, False, used
    )
    own_records(
        own_ref, xrec, feat, tiles_blk, tiles,
        lambda tile, cells: jnp.zeros((1, cells.shape[1]), jnp.float32),
    )

    def bias(tile, start, cells):
        return (spread(rp_ref, tile, blocks, tiles_blk) - sum_squares(cells) / feat) * to_score

    other_records(prev_ref.at[near_side(False)], yrec, build, feat, tiles_blk, tiles, bias)
    ext_records(prog_ref.at[near_side(False)], ext, progs, tiles_blk, tiles)
    high[...] = jnp.full_like(high, NEG)
    total[...] = jnp.zeros_like(total)
    acc[...] = jnp.zeros_like(acc)

    def group(index, carry):
        for step in range(UNROLL):
            at = index * UNROLL + step
            col, row = mine[at], other[at]
            scores = scores_of(yrec, xrec, col, row)
            old = high[col]
            new = jnp.maximum(old, jnp.max(scores, axis=0, keepdims=True))
            weight = jnp.exp2(scores - new)
            part = jnp.sum(weight, axis=0, keepdims=True)
            shrink = jnp.exp2(old - new)
            sums = jnp.dot(ext[row], weight.astype(jnp.bfloat16), preferred_element_type=jnp.float32)
            acc[col] = acc[col] * shrink + sums
            total[col] = total[col] * shrink + part
            high[col] = new
        return carry

    lax.fori_loop(0, groups, group, 0)
    for tile in range(tiles):
        cells = own_ref[tile // tiles_blk, tile % tiles_blk].astype(jnp.float32)
        filled = total[tile] > 0.0
        score = high[tile] + jnp.log2(total[tile]) - sum_squares(cells) * (to_score / feat)
        cp_ref[tile // tiles_blk, tile % tiles_blk : tile % tiles_blk + 1, :] = jnp.where(filled, score * (-EPSILON * LN2), 0.0)
        back_ref[tile] = jnp.where(filled, acc[tile] / total[tile], 0.0)


def plan_kernel(dims, lists_ref, own_ref, next_ref, rp_ref, cp_ref, prog_ref, back_ref, out_ref,
                xrec, yrec, build, ext, acc, mine, other):
    feat, blocks, tiles_blk, most = dims
    tiles = blocks * tiles_blk
    to_score = LOG2E / EPSILON
    progs = prog_ref.shape[2]
    groups = listed_pairs(lists_ref, mine, other, most, blocks, tiles_blk, tiles, True)
    own_records(
        own_ref, xrec, feat, tiles_blk, tiles,
        lambda tile, cells: (rp_ref[tile // tiles_blk, pl.ds(tile % tiles_blk, 1), :] - sum_squares(cells) / feat) * to_score,
    )

    def bias(tile, start, cells):
        return (spread(cp_ref, tile, blocks, tiles_blk) - sum_squares(cells) / feat) * to_score

    other_records(next_ref.at[near_side(True)], yrec, build, feat, tiles_blk, tiles, bias)
    ext_records(prog_ref.at[near_side(True)], ext, progs, tiles_blk, tiles)
    acc[...] = back_ref[...]

    def group(index, carry):
        for step in range(UNROLL):
            at = index * UNROLL + step
            row, col = mine[at], other[at]
            plan = jnp.exp2(scores_of(yrec, xrec, row, col)).astype(jnp.bfloat16)
            acc[row] = acc[row] + jnp.dot(ext[col], plan, preferred_element_type=jnp.float32)
        return carry

    lax.fori_loop(0, groups, group, 0)
    for tile in range(tiles):
        sums = acc[tile]
        out_ref[tile // tiles_blk, tile % tiles_blk] = (sums[0:progs] / sums[progs : progs + 1]).astype(jnp.bfloat16)


MESH = pl.DeviceIdType.MESH


def greet(targets):
    barrier = pltpu.get_barrier_semaphore()
    expected = jnp.int32(0)
    for used, sec, blk in targets:

        @pl.when(used)
        def _():
            pl.semaphore_signal(barrier, inc=1, device_id=(sec, blk), device_id_type=MESH)

        expected = expected + jnp.where(used, 1, 0)
    pl.semaphore_wait(barrier, expected)


def send(src, dst, sems, place, sec, blk):
    return pltpu.make_async_remote_copy(
        src_ref=src, dst_ref=dst, send_sem=sems[0].at[place], recv_sem=sems[1].at[place],
        device_id=(sec, blk), device_id_type=MESH,
    )


STAGES = 8


def gather_kernel(counts, x_ref, prog_ref, pot_ref, list_ref, own_ref, xs_ref, progs_ref, pots_ref, lists_ref,
                  all_lists_ref, send_sem, recv_sem, mate_send, mate_recv):
    n_sec, blocks = counts
    sec, blk = lax.axis_index("sec"), lax.axis_index("blk")
    even = sec % 2 == 0
    partner = jnp.where(even, sec + 1, sec - 1)
    relay_to = jnp.where(even, sec + 2, sec - 2)
    relay_from = jnp.where(even, sec - 2, sec + 2)
    has_to = jnp.logical_and(relay_to >= 0, relay_to < n_sec)
    has_from = jnp.logical_and(relay_from >= 0, relay_from < n_sec)
    core = blk + 1 - 2 * (blk % 2)
    across = (blk + 2) % blocks
    corner = core + 2 - 4 * (core // 2)
    mates = (core, across, corner)
    yes = sec >= 0
    greet(
        [(yes, partner, blk), (has_to, relay_to, blk), (has_from, relay_from, blk)]
        + [(yes, sec, mate) for mate in mates]
    )
    sems, mate_sems = (send_sem, recv_sem), (mate_send, mate_recv)
    width = TILE // blocks
    tiles_blk = x_ref.shape[1] // TILE
    half = x_ref.shape[1] // 2
    sources = [
        (list_ref, lists_ref, None), (x_ref, xs_ref, 0), (x_ref, xs_ref, 1), (prog_ref, progs_ref, 0), (prog_ref, progs_ref, 1),
    ]

    def cut(ref, part):
        return ref if part is None else ref.at[:, part * half : (part + 1) * half]

    def place_of(buffer, side, owner, part):
        return cut(buffer.at[side, owner], part)

    def first(c):
        src, buffer, part = sources[c]
        return send(cut(src, part), place_of(buffer, 0, blk, part), sems, STAGES * c, partner, blk)

    def relay(c):
        _, buffer, part = sources[c]
        return send(
            place_of(buffer, 0, blk, part), place_of(buffer, 1, blk, part), sems, STAGES * c + 1, relay_to, blk
        )

    def share(c, side, kind):
        _, buffer, part = sources[c]
        owner = across if kind == 2 else blk
        slot = place_of(buffer, side, owner, part)
        return send(slot, slot, sems, STAGES * c + 2 + 3 * side + kind, sec, across if kind == 0 else core)

    def to_mate(k):
        mate = mates[k]
        copies = []
        for tile in range(tiles_blk):
            start = pl.multiple_of(tile * TILE + mate * width, width)
            copies.append((x_ref.at[:, pl.ds(start, width)], own_ref.at[blk, tile]))
        copies.append((pot_ref, pots_ref.at[blk]))
        copies.append((list_ref, all_lists_ref.at[blk]))
        per = len(copies)
        return [send(src, dst, mate_sems, per * k + n, sec, mate) for n, (src, dst) in enumerate(copies)]

    chunks = range(len(sources))
    for c in chunks:
        first(c).start()
    for k in range(3):
        for copy in to_mate(k):
            copy.start()
    for tile in range(tiles_blk):
        start = pl.multiple_of(tile * TILE + blk * width, width)
        own_ref[blk, tile] = x_ref[:, pl.ds(start, width)]
    pots_ref[blk] = pot_ref[...]
    all_lists_ref[blk] = list_ref[...]
    for c in chunks:
        first(c).wait_recv()

        @pl.when(has_to)
        def _():
            relay(c).start()

        share(c, 0, 0).start()
        share(c, 0, 1).start()
    for c in chunks:
        share(c, 0, 0).wait_recv()
        share(c, 0, 2).start()

        @pl.when(has_from)
        def _():
            relay(c).wait_recv()
            share(c, 1, 0).start()
            share(c, 1, 1).start()

    @pl.when(has_from)
    def _():
        for c in chunks:
            share(c, 1, 0).wait_recv()
            share(c, 1, 2).start()

    for c in chunks:
        for kind in (1, 2):
            share(c, 0, kind).wait_recv()

    @pl.when(has_from)
    def _():
        for c in chunks:
            for kind in (1, 2):
                share(c, 1, kind).wait_recv()

    for k in range(3):
        for copy in to_mate(k):
            copy.wait_recv()
    for c in chunks:
        first(c).wait_send()
        for kind in range(3):
            share(c, 0, kind).wait_send()

    @pl.when(has_to)
    def _():
        for c in chunks:
            relay(c).wait_send()

    @pl.when(has_from)
    def _():
        for c in chunks:
            for kind in range(3):
                share(c, 1, kind).wait_send()

    for k in range(3):
        for copy in to_mate(k):
            copy.wait_send()


def shift_kernel(counts, steps, part_ref, out_ref, send_sem, recv_sem):
    n_sec, blocks = counts
    sec, blk = lax.axis_index("sec"), lax.axis_index("blk")
    to, source = sec + steps, sec - steps
    has_to = jnp.logical_and(to >= 0, to < n_sec)
    has_from = jnp.logical_and(source >= 0, source < n_sec)
    targets = [(blk + turn) % blocks for turn in range(blocks)]
    greet([(has_to, to, mate) for mate in targets] + [(has_from, source, mate) for mate in targets])

    def copy(turn):
        return send(part_ref, out_ref.at[blk], (send_sem, recv_sem), turn, to, targets[turn])

    def arrival(turn):
        slot = out_ref.at[(blk + blocks - turn) % blocks]
        return send(part_ref, slot, (send_sem, recv_sem), turn, to, targets[turn])

    @pl.when(has_to)
    def _():
        for turn in range(blocks):
            copy(turn).start()

    @pl.when(has_from)
    def _():
        for turn in range(blocks):
            arrival(turn).wait_recv()

    @pl.when(jnp.logical_not(has_from))
    def _():
        out_ref[...] = jnp.zeros_like(out_ref)

    @pl.when(has_to)
    def _():
        for turn in range(blocks):
            copy(turn).wait_send()


def return_kernel(counts, smooth_ref, row_ref, col_ref, out_ref, rows_ref, cols_ref, parts, send_sem, recv_sem):
    n_sec, blocks = counts
    sec, blk = lax.axis_index("sec"), lax.axis_index("blk")
    tiles_blk, width = row_ref.shape[1:]
    mates = [(blk + turn) % blocks for turn in range(blocks)]
    greet([(sec >= 0, sec, mate) for mate in mates[1:]])
    sems = (send_sem, recv_sem)
    per = tiles_blk + 1

    def copies(turn, arriving):
        mate = mates[turn]
        owner = (blk + blocks - turn) % blocks if arriving else blk
        pairs = []
        for tile in range(tiles_blk):
            start = pl.multiple_of(tile * TILE + owner * width, width)
            pairs.append((smooth_ref.at[mate, tile], out_ref.at[:, pl.ds(start, width)]))
        pairs.append((row_ref.at[mate], parts.at[owner]))
        return [send(src, dst, sems, per * (turn - 1) + n, sec, mate) for n, (src, dst) in enumerate(pairs)]

    for turn in range(1, blocks):
        for copy in copies(turn, False):
            copy.start()
    for tile in range(tiles_blk):
        start = pl.multiple_of(tile * TILE + blk * width, width)
        out_ref[:, pl.ds(start, width)] = smooth_ref[blk, tile]
    parts[blk] = row_ref[blk]
    for owner in range(blocks):
        for tile in range(tiles_blk):
            start = tile * TILE + owner * width
            cols_ref[:, start : start + width] = col_ref[owner, blk, tile : tile + 1, :]
    for turn in range(1, blocks):
        for copy in copies(turn, True):
            copy.wait_recv()
    for owner in range(blocks):
        for tile in range(tiles_blk):
            start = tile * TILE + owner * width
            rows_ref[:, start : start + width] = parts[owner, tile : tile + 1, :]
    for turn in range(1, blocks):
        for copy in copies(turn, False):
            copy.wait_send()


def in_vmem(count):
    return [pl.BlockSpec(memory_space=pltpu.VMEM)] * count


def exchange(kernel, number, out_shape, operands, scratch):
    outs = jax.tree.map(lambda _: pl.BlockSpec(memory_space=pltpu.VMEM), out_shape)
    return pl.pallas_call(
        kernel, out_shape=out_shape, in_specs=in_vmem(len(operands)), out_specs=outs, scratch_shapes=scratch,
        compiler_params=pltpu.CompilerParams(collective_id=number, has_side_effects=True),
    )(*operands)


def call(kernel, out_shape, operands, scratch):
    outs = jax.tree.map(lambda _: pl.BlockSpec(memory_space=pltpu.VMEM), out_shape)
    return pl.pallas_call(
        kernel, out_shape=out_shape,
        in_specs=[pl.BlockSpec(memory_space=pltpu.SMEM)] + in_vmem(len(operands) - 1),
        out_specs=outs, scratch_shapes=scratch,
    )(*operands)


def body(features, programs, column_pot, tile_pairs, pair_counts):
    feat, cells_blk = features.shape[1:]
    progs = programs.shape[1]
    tiles_blk = cells_blk // TILE
    most = tile_pairs.shape[2]
    blocks, n_sec = lax.axis_size("blk"), lax.axis_size("sec")
    tiles = tiles_blk * blocks
    width = TILE // blocks
    dims = (feat, blocks, tiles_blk, most)
    counts = (n_sec, blocks)
    f32, bf16 = jnp.float32, jnp.bfloat16
    shape = jax.ShapeDtypeStruct
    long = -(-(2 * most + 1) // 128) * 128
    listed = jnp.concatenate([tile_pairs[0], tile_pairs[1], pair_counts], axis=1)
    listed = jnp.pad(listed, ((0, 0), (0, long - listed.shape[1])))
    dma = pltpu.SemaphoreType.DMA
    mate_copies = (blocks - 1) * (tiles_blk + 2)

    own, xs, progs_all, pot, lists_all, lists = exchange(
        functools.partial(gather_kernel, counts), 0,
        (
            shape((blocks, tiles_blk, feat, width), bf16),
            shape((2, blocks, feat, cells_blk), bf16),
            shape((2, blocks, progs, cells_blk), bf16),
            shape((blocks, 1, cells_blk), bf16),
            shape((2, blocks, 1, long), jnp.int32),
            shape((blocks, 1, long), jnp.int32),
        ),
        (features[0], programs[0], column_pot, listed),
        [dma((STAGES * 5,)), dma((STAGES * 5,)), dma((mate_copies,)), dma((mate_copies,))],
    )

    xrec = pltpu.VMEM((tiles, 2 * HALF, width), bf16)
    yrec = pltpu.VMEM(((tiles + 1) * TILE, 2 * HALF), bf16)
    build = pltpu.VMEM((2 * HALF, TILE), f32)
    ext = pltpu.VMEM((tiles + 1, EXT, TILE), bf16)
    stat = pltpu.VMEM((tiles, 1, width), f32)
    acc = pltpu.VMEM((tiles, EXT, width), f32)
    index = pltpu.SMEM((blocks * most + UNROLL,), jnp.int32)
    pots = shape((blocks, tiles_blk, width), f32)
    all_pots = shape((blocks, blocks, tiles_blk, width), f32)
    sums = shape((tiles, EXT, width), f32)
    shift_scratch = [dma((blocks,)), dma((blocks,))]

    row_own = call(
        functools.partial(row_kernel, dims), pots, (lists, own, xs, pot),
        [xrec, yrec, build, stat, stat, index, index],
    )
    row_prev = exchange(functools.partial(shift_kernel, counts, 1), 1, all_pots, (row_own,), shift_scratch)
    col_own, back = call(
        functools.partial(col_kernel, dims), (pots, sums), (lists_all, own, xs, row_prev, progs_all),
        [xrec, yrec, build, ext, stat, stat, acc, index, index],
    )
    col_all = exchange(functools.partial(shift_kernel, counts, -1), 2, all_pots, (col_own,), shift_scratch)
    smooth = call(
        functools.partial(plan_kernel, dims),
        shape((blocks, tiles_blk, progs, width), bf16),
        (lists, own, xs, row_own, col_all, progs_all, back),
        [xrec, yrec, build, ext, acc, index, index],
    )
    return_copies = (blocks - 1) * (tiles_blk + 1)
    smoothed, row_out, col_out = exchange(
        functools.partial(return_kernel, counts), 3,
        (shape((progs, cells_blk), bf16), shape((1, cells_blk), f32), shape((1, cells_blk), f32)),
        (smooth, row_own, col_all),
        [pltpu.VMEM((blocks, tiles_blk, width), f32), dma((return_copies,)), dma((return_copies,))],
    )
    return smoothed[None], row_out, col_out


def solution(mesh):
    in_specs = (
        P("sec", None, "blk"),
        P("sec", None, "blk"),
        P("sec", "blk"),
        P(None, "sec", "blk"),
        P("sec", "blk"),
    )
    out_specs = (P("sec", None, "blk"), P("sec", "blk"), P("sec", "blk"))
    return jax.shard_map(body, mesh=mesh, in_specs=in_specs, out_specs=out_specs, check_vma=False)
```

```python
import functools
import math

import jax
import jax.numpy as jnp
from jax import lax
from jax.experimental import pallas as pl
from jax.experimental.pallas import tpu as pltpu
from jax.sharding import PartitionSpec as P

TILE = 512
EPSILON = 0.05
LOG2E = math.log2(math.e)
LN2 = math.log(2.0)
NEG = -1e30
UNROLL = 2
SPLITS = 2
HALF = 64
EXT = 48


def split3(value):
    hi = value.astype(jnp.bfloat16).astype(jnp.float32)
    rest = value - hi
    mid = rest.astype(jnp.bfloat16).astype(jnp.float32)
    return hi, mid, rest - mid


def rows_of(pieces, width):
    index = lax.broadcasted_iota(jnp.int32, (8, width), 0)
    block = jnp.zeros((8, width), jnp.float32)
    for place, piece in enumerate(pieces):
        block = jnp.where(index == place, piece, block)
    return block


def sum_squares(cells):
    return jnp.sum(cells * cells, axis=0, keepdims=True)


def own_records(own_ref, xrec, feat, tiles_blk, tiles, bias_of):
    width = TILE // SPLITS
    gain = 2.0 * LOG2E / (feat * EPSILON)
    xrec[...] = jnp.zeros_like(xrec)

    def one(tile, carry):
        cells = own_ref[tile // tiles_blk, tile % tiles_blk].astype(jnp.float32)
        scaled = cells * gain
        high = scaled.astype(jnp.bfloat16)
        xrec[tile, 0:feat, :] = high
        xrec[tile, HALF : HALF + feat, :] = (scaled - high.astype(jnp.float32)).astype(jnp.bfloat16)
        bias = split3(bias_of(tile, cells))
        ones = jnp.ones((1, width), jnp.float32)
        aux = rows_of((ones, ones, ones) + bias, width)
        xrec[tile, HALF - 8 : HALF, :] = aux.astype(jnp.bfloat16)
        return carry

    lax.fori_loop(0, tiles, one, 0)


def other_records(other_ref, yrec, build, feat, tiles_blk, tiles, bias_of):
    build[...] = jnp.zeros_like(build)
    ones = jnp.ones((1, TILE), jnp.float32)

    def one(tile, carry):
        start = pl.multiple_of((tile % tiles_blk) * TILE, TILE)
        cells = other_ref[tile // tiles_blk, 0:feat, pl.ds(start, TILE)].astype(jnp.float32)
        build[0:feat, :] = cells
        build[HALF : HALF + feat, :] = cells
        bias = split3(bias_of(tile, start, cells))
        build[HALF - 8 : HALF, :] = rows_of(bias + (ones, ones, ones), TILE)
        yrec[pl.ds(pl.multiple_of(tile * TILE, TILE), TILE), :] = build[...].T.astype(jnp.bfloat16)
        return carry

    lax.fori_loop(0, tiles, one, 0)
    lane = lax.broadcasted_iota(jnp.int32, (TILE, 2 * HALF), 1)
    yrec[tiles * TILE : (tiles + 1) * TILE, :] = jnp.where(lane == HALF - 8, NEG, 0.0).astype(
        jnp.bfloat16
    )


def ext_records(prog_ref, ext, progs, tiles_blk, tiles):
    index = lax.broadcasted_iota(jnp.int32, (EXT - progs, TILE), 0)
    tail = jnp.where(index == 0, 1.0, 0.0).astype(jnp.bfloat16)

    def one(tile, carry):
        start = pl.multiple_of((tile % tiles_blk) * TILE, TILE)
        ext[tile, 0:progs, :] = prog_ref[tile // tiles_blk, :, pl.ds(start, TILE)]
        ext[tile, progs:EXT, :] = tail
        return carry

    lax.fori_loop(0, tiles, one, 0)
    ext[tiles] = jnp.zeros((EXT, TILE), jnp.bfloat16)


def listed_pairs(lists_ref, mine, other, most, blocks, tiles_blk, tiles, own_first, used=True):
    kinds = blocks // SPLITS
    kind = lax.axis_index("blk") // SPLITS

    def of_block(block, place):
        def one(slot, at):
            row = lists_ref[block, 0, slot] + block * tiles_blk
            col = lists_ref[block, 0, most + slot]
            held, across = (row, col) if own_first else (col, row)
            mine[at] = held // kinds
            other[at] = across
            return at + jnp.where(held % kinds == kind, 1, 0)

        return lax.fori_loop(0, jnp.where(used, lists_ref[block, 0, 2 * most], 0), one, place)

    total = lax.fori_loop(0, blocks, of_block, 0)
    last = mine[jnp.maximum(total - 1, 0)]
    for extra in range(UNROLL - 1):
        mine[total + extra] = last
        other[total + extra] = tiles
    return (total + UNROLL - 1) // UNROLL


def scores_of(yrec, xrec, mine, other):
    rows = yrec[pl.ds(pl.multiple_of(other * TILE, TILE), TILE), :]
    return jnp.dot(rows, xrec[mine], preferred_element_type=jnp.float32)


def spread(parts_ref, tile, blocks, tiles_blk):
    kinds = blocks // SPLITS
    first = (tile % kinds) * SPLITS
    place = (tile % tiles_blk) // kinds
    parts = [parts_ref[first + n, tile // tiles_blk, pl.ds(place, 1), :] for n in range(SPLITS)]
    return jnp.concatenate(parts, axis=1)


def near_side(forward):
    odd = lax.axis_index("sec") % 2
    return odd if forward else 1 - odd


def lane_of(owner, place, blocks):
    kinds = blocks // SPLITS
    return (place * kinds + owner // SPLITS) * TILE + (owner % SPLITS) * (TILE // SPLITS)


def row_kernel(dims, lists_ref, own_ref, next_ref, pot_ref, rp_ref, xrec, yrec, build, high, total, mine, other):
    feat, blocks, tiles_blk, most = dims
    tiles = blocks * tiles_blk
    held_blk = tiles_blk * SPLITS // blocks
    held = blocks * held_blk
    to_score = LOG2E / EPSILON
    groups = listed_pairs(lists_ref, mine, other, most, blocks, tiles_blk, tiles, True)
    own_records(
        own_ref, xrec, feat, held_blk, held,
        lambda tile, cells: jnp.zeros((1, cells.shape[1]), jnp.float32),
    )

    def bias(tile, start, cells):
        pot = pot_ref[tile // tiles_blk, :, pl.ds(start, TILE)].astype(jnp.float32)
        return (pot - sum_squares(cells) / feat) * to_score

    other_records(next_ref.at[near_side(True)], yrec, build, feat, tiles_blk, tiles, bias)
    high[...] = jnp.full_like(high, NEG)
    total[...] = jnp.zeros_like(total)

    def group(index, carry):
        for step in range(UNROLL):
            at = index * UNROLL + step
            row = mine[at]
            scores = scores_of(yrec, xrec, row, other[at])
            old = high[row]
            new = jnp.maximum(old, jnp.max(scores, axis=0, keepdims=True))
            part = jnp.sum(jnp.exp2(scores - new), axis=0, keepdims=True)
            total[row] = total[row] * jnp.exp2(old - new) + part
            high[row] = new
        return carry

    lax.fori_loop(0, groups, group, 0)
    at_end = lax.axis_index("sec") == lax.axis_size("sec") - 1
    for tile in range(held):
        cells = own_ref[tile // held_blk, tile % held_blk].astype(jnp.float32)
        score = high[tile] + jnp.log2(total[tile]) - sum_squares(cells) * (to_score / feat)
        rp_ref[tile // held_blk, tile % held_blk : tile % held_blk + 1, :] = jnp.where(at_end, 0.0, score * (-EPSILON * LN2))


def col_kernel(dims, lists_ref, own_ref, prev_ref, rp_ref, prog_ref, cp_ref, back_ref,
               xrec, yrec, build, ext, high, total, acc, mine, other):
    feat, blocks, tiles_blk, most = dims
    tiles = blocks * tiles_blk
    held_blk = tiles_blk * SPLITS // blocks
    held = blocks * held_blk
    to_score = LOG2E / EPSILON
    progs = prog_ref.shape[2]
    used = lax.axis_index("sec") > 0
    groups = listed_pairs(
        lists_ref.at[near_side(False)], mine, other, most, blocks, tiles_blk, tiles, False, used
    )
    own_records(
        own_ref, xrec, feat, held_blk, held,
        lambda tile, cells: jnp.zeros((1, cells.shape[1]), jnp.float32),
    )

    def bias(tile, start, cells):
        return (spread(rp_ref, tile, blocks, tiles_blk) - sum_squares(cells) / feat) * to_score

    other_records(prev_ref.at[near_side(False)], yrec, build, feat, tiles_blk, tiles, bias)
    ext_records(prog_ref.at[near_side(False)], ext, progs, tiles_blk, tiles)
    high[...] = jnp.full_like(high, NEG)
    total[...] = jnp.zeros_like(total)
    acc[...] = jnp.zeros_like(acc)

    def group(index, carry):
        for step in range(UNROLL):
            at = index * UNROLL + step
            col, row = mine[at], other[at]
            scores = scores_of(yrec, xrec, col, row)
            old = high[col]
            new = jnp.maximum(old, jnp.max(scores, axis=0, keepdims=True))
            weight = jnp.exp2(scores - new)
            part = jnp.sum(weight, axis=0, keepdims=True)
            shrink = jnp.exp2(old - new)
            sums = jnp.dot(ext[row], weight.astype(jnp.bfloat16), preferred_element_type=jnp.float32)
            acc[col] = acc[col] * shrink + sums
            total[col] = total[col] * shrink + part
            high[col] = new
        return carry

    lax.fori_loop(0, groups, group, 0)
    for tile in range(held):
        cells = own_ref[tile // held_blk, tile % held_blk].astype(jnp.float32)
        filled = total[tile] > 0.0
        score = high[tile] + jnp.log2(total[tile]) - sum_squares(cells) * (to_score / feat)
        cp_ref[tile // held_blk, tile % held_blk : tile % held_blk + 1, :] = jnp.where(filled, score * (-EPSILON * LN2), 0.0)
        back_ref[tile] = jnp.where(filled, acc[tile] / total[tile], 0.0)


def plan_kernel(dims, lists_ref, own_ref, next_ref, rp_ref, cp_ref, prog_ref, back_ref, home_ref, out_ref, rows_ref, cols_ref,
                xrec, yrec, build, ext, acc, mine, other):
    feat, blocks, tiles_blk, most = dims
    tiles = blocks * tiles_blk
    held_blk = tiles_blk * SPLITS // blocks
    held = blocks * held_blk
    to_score = LOG2E / EPSILON
    progs = prog_ref.shape[2]
    groups = listed_pairs(lists_ref, mine, other, most, blocks, tiles_blk, tiles, True)
    own_records(
        own_ref, xrec, feat, held_blk, held,
        lambda tile, cells: (rp_ref[tile // held_blk, pl.ds(tile % held_blk, 1), :] - sum_squares(cells) / feat) * to_score,
    )

    def bias(tile, start, cells):
        return (spread(cp_ref, tile, blocks, tiles_blk) - sum_squares(cells) / feat) * to_score

    other_records(next_ref.at[near_side(True)], yrec, build, feat, tiles_blk, tiles, bias)
    ext_records(prog_ref.at[near_side(True)], ext, progs, tiles_blk, tiles)
    acc[...] = back_ref[...]
    width = TILE // SPLITS
    for owner in range(blocks):
        for place in range(held_blk):
            start = lane_of(owner, place, blocks)
            rows_ref[:, start : start + width] = home_ref[owner, place : place + 1, :]
            cols_ref[:, start : start + width] = cp_ref[owner, lax.axis_index("blk"), place : place + 1, :]

    def group(index, carry):
        for step in range(UNROLL):
            at = index * UNROLL + step
            row, col = mine[at], other[at]
            plan = jnp.exp2(scores_of(yrec, xrec, row, col)).astype(jnp.bfloat16)
            acc[row] = acc[row] + jnp.dot(ext[col], plan, preferred_element_type=jnp.float32)
        return carry

    lax.fori_loop(0, groups, group, 0)
    for tile in range(held):
        sums = acc[tile]
        out_ref[tile // held_blk, tile % held_blk] = (sums[0:progs] / sums[progs : progs + 1]).astype(jnp.bfloat16)


MESH = pl.DeviceIdType.MESH


def greet(targets):
    barrier = pltpu.get_barrier_semaphore()
    expected = jnp.int32(0)
    for used, sec, blk in targets:

        @pl.when(used)
        def _():
            pl.semaphore_signal(barrier, inc=1, device_id=(sec, blk), device_id_type=MESH)

        expected = expected + jnp.where(used, 1, 0)
    pl.semaphore_wait(barrier, expected)


def send(src, dst, sems, place, sec, blk):
    return pltpu.make_async_remote_copy(
        src_ref=src, dst_ref=dst, send_sem=sems[0].at[place], recv_sem=sems[1].at[place],
        device_id=(sec, blk), device_id_type=MESH,
    )


STAGES = 8


def gather_kernel(counts, x_ref, prog_ref, pot_ref, list_ref, own_ref, xs_ref, progs_ref, pots_ref, lists_ref,
                  all_lists_ref, send_sem, recv_sem, mate_send, mate_recv):
    n_sec, blocks = counts
    sec, blk = lax.axis_index("sec"), lax.axis_index("blk")
    even = sec % 2 == 0
    partner = jnp.where(even, sec + 1, sec - 1)
    relay_to = jnp.where(even, sec + 2, sec - 2)
    relay_from = jnp.where(even, sec - 2, sec + 2)
    has_to = jnp.logical_and(relay_to >= 0, relay_to < n_sec)
    has_from = jnp.logical_and(relay_from >= 0, relay_from < n_sec)
    core = blk + 1 - 2 * (blk % 2)
    across = (blk + 2) % blocks
    corner = core + 2 - 4 * (core // 2)
    mates = (core, across, corner)
    yes = sec >= 0
    greet(
        [(yes, partner, blk), (has_to, relay_to, blk), (has_from, relay_from, blk)]
        + [(yes, sec, mate) for mate in mates]
    )
    sems, mate_sems = (send_sem, recv_sem), (mate_send, mate_recv)
    width = TILE // SPLITS
    held_blk = x_ref.shape[1] // TILE * SPLITS // blocks
    half = x_ref.shape[1] // 2
    sources = [
        (list_ref, lists_ref, None), (x_ref, xs_ref, 0), (x_ref, xs_ref, 1), (prog_ref, progs_ref, 0), (prog_ref, progs_ref, 1),
    ]

    def cut(ref, part):
        return ref if part is None else ref.at[:, part * half : (part + 1) * half]

    def place_of(buffer, side, owner, part):
        return cut(buffer.at[side, owner], part)

    def first(c):
        src, buffer, part = sources[c]
        return send(cut(src, part), place_of(buffer, 0, blk, part), sems, STAGES * c, partner, blk)

    def relay(c):
        _, buffer, part = sources[c]
        return send(
            place_of(buffer, 0, blk, part), place_of(buffer, 1, blk, part), sems, STAGES * c + 1, relay_to, blk
        )

    def share(c, side, kind):
        _, buffer, part = sources[c]
        owner = across if kind == 2 else blk
        slot = place_of(buffer, side, owner, part)
        return send(slot, slot, sems, STAGES * c + 2 + 3 * side + kind, sec, across if kind == 0 else core)

    def to_mate(k):
        mate = mates[k]
        copies = []
        for tile in range(held_blk):
            start = pl.multiple_of(lane_of(mate, tile, blocks), width)
            copies.append((x_ref.at[:, pl.ds(start, width)], own_ref.at[blk, tile]))
        copies.append((pot_ref, pots_ref.at[blk]))
        copies.append((list_ref, all_lists_ref.at[blk]))
        per = len(copies)
        return [send(src, dst, mate_sems, per * k + n, sec, mate) for n, (src, dst) in enumerate(copies)]

    chunks = range(len(sources))
    for c in chunks:
        first(c).start()
    for k in range(3):
        for copy in to_mate(k):
            copy.start()
    for tile in range(held_blk):
        start = pl.multiple_of(lane_of(blk, tile, blocks), width)
        own_ref[blk, tile] = x_ref[:, pl.ds(start, width)]
    pots_ref[blk] = pot_ref[...]
    all_lists_ref[blk] = list_ref[...]
    for c in chunks:
        first(c).wait_recv()

        @pl.when(has_to)
        def _():
            relay(c).start()

        share(c, 0, 0).start()
        share(c, 0, 1).start()
    for c in chunks:
        share(c, 0, 0).wait_recv()
        share(c, 0, 2).start()

        @pl.when(has_from)
        def _():
            relay(c).wait_recv()
            share(c, 1, 0).start()
            share(c, 1, 1).start()

    @pl.when(has_from)
    def _():
        for c in chunks:
            share(c, 1, 0).wait_recv()
            share(c, 1, 2).start()

    for c in chunks:
        for kind in (1, 2):
            share(c, 0, kind).wait_recv()

    @pl.when(has_from)
    def _():
        for c in chunks:
            for kind in (1, 2):
                share(c, 1, kind).wait_recv()

    for k in range(3):
        for copy in to_mate(k):
            copy.wait_recv()
    for c in chunks:
        first(c).wait_send()
        for kind in range(3):
            share(c, 0, kind).wait_send()

    @pl.when(has_to)
    def _():
        for c in chunks:
            relay(c).wait_send()

    @pl.when(has_from)
    def _():
        for c in chunks:
            for kind in range(3):
                share(c, 1, kind).wait_send()

    for k in range(3):
        for copy in to_mate(k):
            copy.wait_send()


def shift_kernel(counts, steps, home, part_ref, out_ref, *rest):
    home_ref = rest[0] if home else None
    send_sem, recv_sem = rest[-2:]
    n_sec, blocks = counts
    sec, blk = lax.axis_index("sec"), lax.axis_index("blk")
    to, source = sec + steps, sec - steps
    has_to = jnp.logical_and(to >= 0, to < n_sec)
    has_from = jnp.logical_and(source >= 0, source < n_sec)
    targets = [(blk + turn) % blocks for turn in range(blocks)]
    mates = [(sec >= 0, sec, mate) for mate in targets[1:]] if home else []
    greet(mates + [(has_to, to, mate) for mate in targets] + [(has_from, source, mate) for mate in targets])

    def copy(turn):
        return send(part_ref, out_ref.at[blk], (send_sem, recv_sem), turn, to, targets[turn])

    def homeward(turn, owner):
        src = part_ref.at[targets[turn]]
        return send(src, home_ref.at[owner], (send_sem, recv_sem), blocks + turn - 1, sec, targets[turn])

    def arrival(turn):
        slot = out_ref.at[(blk + blocks - turn) % blocks]
        return send(part_ref, slot, (send_sem, recv_sem), turn, to, targets[turn])

    @pl.when(has_to)
    def _():
        for turn in range(blocks):
            copy(turn).start()

    if home:
        for turn in range(1, blocks):
            homeward(turn, blk).start()
        home_ref[blk] = part_ref[blk]
        for turn in range(1, blocks):
            homeward(turn, (blk + blocks - turn) % blocks).wait_recv()

    @pl.when(has_from)
    def _():
        for turn in range(blocks):
            arrival(turn).wait_recv()

    @pl.when(jnp.logical_not(has_from))
    def _():
        out_ref[...] = jnp.zeros_like(out_ref)

    @pl.when(has_to)
    def _():
        for turn in range(blocks):
            copy(turn).wait_send()

    if home:
        for turn in range(1, blocks):
            homeward(turn, blk).wait_send()


def return_kernel(counts, smooth_ref, out_ref, send_sem, recv_sem):
    n_sec, blocks = counts
    sec, blk = lax.axis_index("sec"), lax.axis_index("blk")
    held_blk, width = smooth_ref.shape[1], smooth_ref.shape[3]
    mates = [(blk + turn) % blocks for turn in range(blocks)]
    greet([(sec >= 0, sec, mate) for mate in mates[1:]])

    def copies(turn, owner):
        found = []
        for place in range(held_blk):
            start = pl.multiple_of(lane_of(owner, place, blocks), width)
            src, dst = smooth_ref.at[mates[turn], place], out_ref.at[:, pl.ds(start, width)]
            found.append(send(src, dst, (send_sem, recv_sem), held_blk * (turn - 1) + place, sec, mates[turn]))
        return found

    for turn in range(1, blocks):
        for copy in copies(turn, blk):
            copy.start()
    for place in range(held_blk):
        start = pl.multiple_of(lane_of(blk, place, blocks), width)
        out_ref[:, pl.ds(start, width)] = smooth_ref[blk, place]
    for turn in range(1, blocks):
        for copy in copies(turn, (blk + blocks - turn) % blocks):
            copy.wait_recv()
    for turn in range(1, blocks):
        for copy in copies(turn, blk):
            copy.wait_send()


def in_vmem(count):
    return [pl.BlockSpec(memory_space=pltpu.VMEM)] * count


def exchange(kernel, number, out_shape, operands, scratch):
    outs = jax.tree.map(lambda _: pl.BlockSpec(memory_space=pltpu.VMEM), out_shape)
    return pl.pallas_call(
        kernel, out_shape=out_shape, in_specs=in_vmem(len(operands)), out_specs=outs, scratch_shapes=scratch,
        compiler_params=pltpu.CompilerParams(collective_id=number, has_side_effects=True),
    )(*operands)


def call(kernel, out_shape, operands, scratch):
    outs = jax.tree.map(lambda _: pl.BlockSpec(memory_space=pltpu.VMEM), out_shape)
    return pl.pallas_call(
        kernel, out_shape=out_shape,
        in_specs=[pl.BlockSpec(memory_space=pltpu.SMEM)] + in_vmem(len(operands) - 1),
        out_specs=outs, scratch_shapes=scratch,
    )(*operands)


def body(features, programs, column_pot, tile_pairs, pair_counts):
    feat, cells_blk = features.shape[1:]
    progs = programs.shape[1]
    tiles_blk = cells_blk // TILE
    most = tile_pairs.shape[2]
    blocks, n_sec = lax.axis_size("blk"), lax.axis_size("sec")
    tiles = tiles_blk * blocks
    width = TILE // SPLITS
    held_blk = tiles_blk * SPLITS // blocks
    held = blocks * held_blk
    dims = (feat, blocks, tiles_blk, most)
    counts = (n_sec, blocks)
    f32, bf16 = jnp.float32, jnp.bfloat16
    shape = jax.ShapeDtypeStruct
    long = -(-(2 * most + 1) // 128) * 128
    listed = jnp.concatenate([tile_pairs[0], tile_pairs[1], pair_counts], axis=1)
    listed = jnp.pad(listed, ((0, 0), (0, long - listed.shape[1])))
    dma = pltpu.SemaphoreType.DMA
    mate_copies = (blocks - 1) * (held_blk + 2)

    own, xs, progs_all, pot, lists_all, lists = exchange(
        functools.partial(gather_kernel, counts), 0,
        (
            shape((blocks, held_blk, feat, width), bf16),
            shape((2, blocks, feat, cells_blk), bf16),
            shape((2, blocks, progs, cells_blk), bf16),
            shape((blocks, 1, cells_blk), bf16),
            shape((2, blocks, 1, long), jnp.int32),
            shape((blocks, 1, long), jnp.int32),
        ),
        (features[0], programs[0], column_pot, listed),
        [dma((STAGES * 5,)), dma((STAGES * 5,)), dma((mate_copies,)), dma((mate_copies,))],
    )

    xrec = pltpu.VMEM((held, 2 * HALF, width), bf16)
    yrec = pltpu.VMEM(((tiles + 1) * TILE, 2 * HALF), bf16)
    build = pltpu.VMEM((2 * HALF, TILE), f32)
    ext = pltpu.VMEM((tiles + 1, EXT, TILE), bf16)
    stat = pltpu.VMEM((held, 1, width), f32)
    acc = pltpu.VMEM((held, EXT, width), f32)
    index = pltpu.SMEM((blocks * most + UNROLL,), jnp.int32)
    pots = shape((blocks, held_blk, width), f32)
    all_pots = shape((blocks, blocks, held_blk, width), f32)
    sums = shape((held, EXT, width), f32)

    row_own = call(
        functools.partial(row_kernel, dims), pots, (lists, own, xs, pot),
        [xrec, yrec, build, stat, stat, index, index],
    )
    row_prev, row_home = exchange(
        functools.partial(shift_kernel, counts, 1, True), 1, (all_pots, pots), (row_own,),
        [dma((2 * blocks - 1,)), dma((2 * blocks - 1,))],
    )
    col_own, back = call(
        functools.partial(col_kernel, dims), (pots, sums), (lists_all, own, xs, row_prev, progs_all),
        [xrec, yrec, build, ext, stat, stat, acc, index, index],
    )
    col_all = exchange(
        functools.partial(shift_kernel, counts, -1, False), 2, all_pots, (col_own,), [dma((blocks,)), dma((blocks,))]
    )
    line = shape((1, cells_blk), f32)
    smooth, row_out, col_out = call(
        functools.partial(plan_kernel, dims),
        (shape((blocks, held_blk, progs, width), bf16), line, line),
        (lists, own, xs, row_own, col_all, progs_all, back, row_home),
        [xrec, yrec, build, ext, acc, index, index],
    )
    return_copies = (blocks - 1) * held_blk
    smoothed = exchange(
        functools.partial(return_kernel, counts), 3, shape((progs, cells_blk), bf16), (smooth,),
        [dma((return_copies,)), dma((return_copies,))],
    )
    return smoothed[None], row_out, col_out


def solution(mesh):
    in_specs = (
        P("sec", None, "blk"),
        P("sec", None, "blk"),
        P("sec", "blk"),
        P(None, "sec", "blk"),
        P("sec", "blk"),
    )
    out_specs = (P("sec", None, "blk"), P("sec", "blk"), P("sec", "blk"))
    return jax.shard_map(body, mesh=mesh, in_specs=in_specs, out_specs=out_specs, check_vma=False)
```

```python
import functools
import math

import jax
import jax.numpy as jnp
from jax import lax
from jax.experimental import pallas as pl
from jax.experimental.pallas import tpu as pltpu
from jax.sharding import PartitionSpec as P

TILE = 512
EPSILON = 0.05
LOG2E = math.log2(math.e)
LN2 = math.log(2.0)
NEG = -1e30
UNROLL = 2
SPLITS = 2
HALF = 64
EXT = 48


def split3(value):
    hi = value.astype(jnp.bfloat16).astype(jnp.float32)
    rest = value - hi
    mid = rest.astype(jnp.bfloat16).astype(jnp.float32)
    return hi, mid, rest - mid


def rows_of(pieces, width):
    index = lax.broadcasted_iota(jnp.int32, (8, width), 0)
    block = jnp.zeros((8, width), jnp.float32)
    for place, piece in enumerate(pieces):
        block = jnp.where(index == place, piece, block)
    return block


def sum_squares(cells):
    return jnp.sum(cells * cells, axis=0, keepdims=True)


def own_records(own_ref, xrec, feat, tiles_blk, tiles, bias_of):
    width = TILE // SPLITS
    gain = 2.0 * LOG2E / (feat * EPSILON)
    xrec[...] = jnp.zeros_like(xrec)

    def one(tile, carry):
        cells = own_ref[tile // tiles_blk, tile % tiles_blk].astype(jnp.float32)
        scaled = cells * gain
        high = scaled.astype(jnp.bfloat16)
        xrec[tile, 0:feat, :] = high
        xrec[tile, HALF : HALF + feat, :] = (scaled - high.astype(jnp.float32)).astype(jnp.bfloat16)
        bias = split3(bias_of(tile, cells))
        ones = jnp.ones((1, width), jnp.float32)
        aux = rows_of((ones, ones, ones) + bias, width)
        xrec[tile, HALF - 8 : HALF, :] = aux.astype(jnp.bfloat16)
        return carry

    lax.fori_loop(0, tiles, one, 0)


def other_records(other_ref, yrec, build, feat, tiles_blk, tiles, bias_of):
    build[...] = jnp.zeros_like(build)
    ones = jnp.ones((1, TILE), jnp.float32)

    def one(tile, carry):
        start = pl.multiple_of((tile % tiles_blk) * TILE, TILE)
        cells = other_ref[tile // tiles_blk, 0:feat, pl.ds(start, TILE)].astype(jnp.float32)
        build[0:feat, :] = cells
        build[HALF : HALF + feat, :] = cells
        bias = split3(bias_of(tile, start, cells))
        build[HALF - 8 : HALF, :] = rows_of(bias + (ones, ones, ones), TILE)
        yrec[pl.ds(pl.multiple_of(tile * TILE, TILE), TILE), :] = build[...].T.astype(jnp.bfloat16)
        return carry

    lax.fori_loop(0, tiles, one, 0)
    lane = lax.broadcasted_iota(jnp.int32, (TILE, 2 * HALF), 1)
    yrec[tiles * TILE : (tiles + 1) * TILE, :] = jnp.where(lane == HALF - 8, NEG, 0.0).astype(
        jnp.bfloat16
    )


def ext_records(prog_ref, ext, progs, tiles_blk, tiles):
    index = lax.broadcasted_iota(jnp.int32, (EXT - progs, TILE), 0)
    tail = jnp.where(index == 0, 1.0, 0.0).astype(jnp.bfloat16)

    def one(tile, carry):
        start = pl.multiple_of((tile % tiles_blk) * TILE, TILE)
        ext[tile, 0:progs, :] = prog_ref[tile // tiles_blk, :, pl.ds(start, TILE)]
        ext[tile, progs:EXT, :] = tail
        return carry

    lax.fori_loop(0, tiles, one, 0)
    ext[tiles] = jnp.zeros((EXT, TILE), jnp.bfloat16)


def listed_pairs(lists_ref, mine, other, most, blocks, tiles_blk, tiles, own_first, used=True):
    kinds = blocks // SPLITS
    kind = lax.axis_index("blk") // SPLITS

    def of_block(block, place):
        def one(slot, at):
            row = lists_ref[block, 0, slot] + block * tiles_blk
            col = lists_ref[block, 0, most + slot]
            held, across = (row, col) if own_first else (col, row)
            mine[at] = held // kinds
            other[at] = across
            return at + jnp.where(held % kinds == kind, 1, 0)

        return lax.fori_loop(0, jnp.where(used, lists_ref[block, 0, 2 * most], 0), one, place)

    total = lax.fori_loop(0, blocks, of_block, 0)
    last = jnp.where(total > 0, mine[jnp.maximum(total - 1, 0)], 0)
    for extra in range(2 * UNROLL):
        mine[total + extra] = last
        other[total + extra] = tiles
    return (total + UNROLL - 1) // UNROLL


def scores_of(yrec, xrec, mine, other):
    rows = yrec[pl.ds(pl.multiple_of(other * TILE, TILE), TILE), :]
    return jnp.dot(rows, xrec[mine], preferred_element_type=jnp.float32)


def over_pairs(groups, ready, tops, yrec, xrec, mine, other, use):
    def make(at, place):
        scores = scores_of(yrec, xrec, mine[at], other[at])
        ready[place][...] = scores
        if tops is not None:
            tops[place] = jnp.max(scores, axis=0, keepdims=True)

    make(0, 0)

    def group(index, carry):
        for step in range(UNROLL):
            at = index * UNROLL + step
            make(at + 1, (step + 1) % UNROLL)
            use(ready[step], None if tops is None else tops[step], mine[at], other[at])
        return carry

    lax.fori_loop(0, groups, group, 0)


def spread(parts_ref, tile, blocks, tiles_blk):
    kinds = blocks // SPLITS
    first = (tile % kinds) * SPLITS
    place = (tile % tiles_blk) // kinds
    parts = [parts_ref[first + n, tile // tiles_blk, pl.ds(place, 1), :] for n in range(SPLITS)]
    return jnp.concatenate(parts, axis=1)


def near_side(forward):
    odd = lax.axis_index("sec") % 2
    return odd if forward else 1 - odd


def lane_of(owner, place, blocks):
    kinds = blocks // SPLITS
    return (place * kinds + owner // SPLITS) * TILE + (owner % SPLITS) * (TILE // SPLITS)


def row_kernel(dims, lists_ref, own_ref, next_ref, pot_ref, rp_ref, xrec, yrec, build, high, total, mine, other, *ready):
    feat, blocks, tiles_blk, most = dims
    tiles = blocks * tiles_blk
    held_blk = tiles_blk * SPLITS // blocks
    held = blocks * held_blk
    to_score = LOG2E / EPSILON
    groups = listed_pairs(lists_ref, mine, other, most, blocks, tiles_blk, tiles, True)
    own_records(
        own_ref, xrec, feat, held_blk, held,
        lambda tile, cells: jnp.zeros((1, cells.shape[1]), jnp.float32),
    )

    def bias(tile, start, cells):
        pot = pot_ref[tile // tiles_blk, :, pl.ds(start, TILE)].astype(jnp.float32)
        return (pot - sum_squares(cells) / feat) * to_score

    other_records(next_ref.at[near_side(True)], yrec, build, feat, tiles_blk, tiles, bias)
    high[...] = jnp.full_like(high, NEG)
    total[...] = jnp.zeros_like(total)

    def use(scores_ref, top, row, col):
        old = high[row]
        new = jnp.maximum(old, jnp.max(scores_ref[...], axis=0, keepdims=True))
        part = jnp.sum(jnp.exp2(scores_ref[...] - new), axis=0, keepdims=True)
        total[row] = total[row] * jnp.exp2(old - new) + part
        high[row] = new

    over_pairs(groups, ready, None, yrec, xrec, mine, other, use)
    at_end = lax.axis_index("sec") == lax.axis_size("sec") - 1
    for tile in range(held):
        cells = own_ref[tile // held_blk, tile % held_blk].astype(jnp.float32)
        score = high[tile] + jnp.log2(total[tile]) - sum_squares(cells) * (to_score / feat)
        rp_ref[tile // held_blk, tile % held_blk : tile % held_blk + 1, :] = jnp.where(at_end, 0.0, score * (-EPSILON * LN2))


def col_kernel(dims, lists_ref, own_ref, prev_ref, rp_ref, prog_ref, cp_ref, back_ref,
               xrec, yrec, build, ext, high, total, acc, mine, other, tops, *ready):
    feat, blocks, tiles_blk, most = dims
    tiles = blocks * tiles_blk
    held_blk = tiles_blk * SPLITS // blocks
    held = blocks * held_blk
    to_score = LOG2E / EPSILON
    progs = prog_ref.shape[2]
    used = lax.axis_index("sec") > 0
    groups = listed_pairs(
        lists_ref.at[near_side(False)], mine, other, most, blocks, tiles_blk, tiles, False, used
    )
    own_records(
        own_ref, xrec, feat, held_blk, held,
        lambda tile, cells: jnp.zeros((1, cells.shape[1]), jnp.float32),
    )

    def bias(tile, start, cells):
        return (spread(rp_ref, tile, blocks, tiles_blk) - sum_squares(cells) / feat) * to_score

    other_records(prev_ref.at[near_side(False)], yrec, build, feat, tiles_blk, tiles, bias)
    ext_records(prog_ref.at[near_side(False)], ext, progs, tiles_blk, tiles)
    high[...] = jnp.full_like(high, NEG)
    total[...] = jnp.zeros_like(total)
    acc[...] = jnp.zeros_like(acc)

    def use(scores_ref, top, col, row):
        old = high[col]
        new = jnp.maximum(old, top)
        weight = jnp.exp2(scores_ref[...] - new)
        part = jnp.sum(weight, axis=0, keepdims=True)
        shrink = jnp.exp2(old - new)
        sums = jnp.dot(ext[row], weight.astype(jnp.bfloat16), preferred_element_type=jnp.float32)
        acc[col] = acc[col] * shrink + sums
        total[col] = total[col] * shrink + part
        high[col] = new

    over_pairs(groups, ready, tops, yrec, xrec, mine, other, use)
    for tile in range(held):
        cells = own_ref[tile // held_blk, tile % held_blk].astype(jnp.float32)
        filled = total[tile] > 0.0
        score = high[tile] + jnp.log2(total[tile]) - sum_squares(cells) * (to_score / feat)
        cp_ref[tile // held_blk, tile % held_blk : tile % held_blk + 1, :] = jnp.where(filled, score * (-EPSILON * LN2), 0.0)
        back_ref[tile] = jnp.where(filled, acc[tile] / total[tile], 0.0)


def plan_kernel(dims, lists_ref, own_ref, next_ref, rp_ref, cp_ref, prog_ref, back_ref, home_ref, out_ref, rows_ref, cols_ref,
                xrec, yrec, build, ext, acc, mine, other, *ready):
    feat, blocks, tiles_blk, most = dims
    tiles = blocks * tiles_blk
    held_blk = tiles_blk * SPLITS // blocks
    held = blocks * held_blk
    to_score = LOG2E / EPSILON
    progs = prog_ref.shape[2]
    groups = listed_pairs(lists_ref, mine, other, most, blocks, tiles_blk, tiles, True)
    own_records(
        own_ref, xrec, feat, held_blk, held,
        lambda tile, cells: (rp_ref[tile // held_blk, pl.ds(tile % held_blk, 1), :] - sum_squares(cells) / feat) * to_score,
    )

    def bias(tile, start, cells):
        return (spread(cp_ref, tile, blocks, tiles_blk) - sum_squares(cells) / feat) * to_score

    other_records(next_ref.at[near_side(True)], yrec, build, feat, tiles_blk, tiles, bias)
    ext_records(prog_ref.at[near_side(True)], ext, progs, tiles_blk, tiles)
    acc[...] = back_ref[...]
    width = TILE // SPLITS
    for owner in range(blocks):
        for place in range(held_blk):
            start = lane_of(owner, place, blocks)
            rows_ref[:, start : start + width] = home_ref[owner, place : place + 1, :]
            cols_ref[:, start : start + width] = cp_ref[owner, lax.axis_index("blk"), place : place + 1, :]

    def use(scores_ref, top, row, col):
        plan = jnp.exp2(scores_ref[...]).astype(jnp.bfloat16)
        acc[row] = acc[row] + jnp.dot(ext[col], plan, preferred_element_type=jnp.float32)

    over_pairs(groups, ready, None, yrec, xrec, mine, other, use)
    for tile in range(held):
        sums = acc[tile]
        out_ref[tile // held_blk, tile % held_blk] = (sums[0:progs] / sums[progs : progs + 1]).astype(jnp.bfloat16)


MESH = pl.DeviceIdType.MESH


def greet(targets):
    barrier = pltpu.get_barrier_semaphore()
    expected = jnp.int32(0)
    for used, sec, blk in targets:

        @pl.when(used)
        def _():
            pl.semaphore_signal(barrier, inc=1, device_id=(sec, blk), device_id_type=MESH)

        expected = expected + jnp.where(used, 1, 0)
    pl.semaphore_wait(barrier, expected)


def send(src, dst, sems, place, sec, blk):
    return pltpu.make_async_remote_copy(
        src_ref=src, dst_ref=dst, send_sem=sems[0].at[place], recv_sem=sems[1].at[place],
        device_id=(sec, blk), device_id_type=MESH,
    )


STAGES = 8


def gather_kernel(counts, x_ref, prog_ref, pot_ref, list_ref, own_ref, xs_ref, progs_ref, pots_ref, lists_ref,
                  all_lists_ref, send_sem, recv_sem, mate_send, mate_recv):
    n_sec, blocks = counts
    sec, blk = lax.axis_index("sec"), lax.axis_index("blk")
    even = sec % 2 == 0
    partner = jnp.where(even, sec + 1, sec - 1)
    relay_to = jnp.where(even, sec + 2, sec - 2)
    relay_from = jnp.where(even, sec - 2, sec + 2)
    has_to = jnp.logical_and(relay_to >= 0, relay_to < n_sec)
    has_from = jnp.logical_and(relay_from >= 0, relay_from < n_sec)
    core = blk + 1 - 2 * (blk % 2)
    across = (blk + 2) % blocks
    corner = core + 2 - 4 * (core // 2)
    mates = (core, across, corner)
    yes = sec >= 0
    greet(
        [(yes, partner, blk), (has_to, relay_to, blk), (has_from, relay_from, blk)]
        + [(yes, sec, mate) for mate in mates]
    )
    sems, mate_sems = (send_sem, recv_sem), (mate_send, mate_recv)
    width = TILE // SPLITS
    held_blk = x_ref.shape[1] // TILE * SPLITS // blocks
    half = x_ref.shape[1] // 2
    sources = [
        (list_ref, lists_ref, None), (x_ref, xs_ref, 0), (x_ref, xs_ref, 1), (prog_ref, progs_ref, 0), (prog_ref, progs_ref, 1),
    ]

    def cut(ref, part):
        return ref if part is None else ref.at[:, part * half : (part + 1) * half]

    def place_of(buffer, side, owner, part):
        return cut(buffer.at[side, owner], part)

    def first(c):
        src, buffer, part = sources[c]
        return send(cut(src, part), place_of(buffer, 0, blk, part), sems, STAGES * c, partner, blk)

    def relay(c):
        _, buffer, part = sources[c]
        return send(
            place_of(buffer, 0, blk, part), place_of(buffer, 1, blk, part), sems, STAGES * c + 1, relay_to, blk
        )

    def share(c, side, kind):
        _, buffer, part = sources[c]
        owner = across if kind == 2 else blk
        slot = place_of(buffer, side, owner, part)
        return send(slot, slot, sems, STAGES * c + 2 + 3 * side + kind, sec, across if kind == 0 else core)

    def to_mate(k):
        mate = mates[k]
        copies = []
        for tile in range(held_blk):
            start = pl.multiple_of(lane_of(mate, tile, blocks), width)
            copies.append((x_ref.at[:, pl.ds(start, width)], own_ref.at[blk, tile]))
        copies.append((pot_ref, pots_ref.at[blk]))
        copies.append((list_ref, all_lists_ref.at[blk]))
        per = len(copies)
        return [send(src, dst, mate_sems, per * k + n, sec, mate) for n, (src, dst) in enumerate(copies)]

    chunks = range(len(sources))
    for c in chunks:
        first(c).start()
    for k in range(3):
        for copy in to_mate(k):
            copy.start()
    for tile in range(held_blk):
        start = pl.multiple_of(lane_of(blk, tile, blocks), width)
        own_ref[blk, tile] = x_ref[:, pl.ds(start, width)]
    pots_ref[blk] = pot_ref[...]
    all_lists_ref[blk] = list_ref[...]
    for turn in range(len(sources) + 2):
        if turn in chunks:
            first(turn).wait_recv()

            @pl.when(has_to)
            def _():
                relay(turn).start()

            share(turn, 0, 0).start()
            share(turn, 0, 1).start()
        if turn - 1 in chunks:
            share(turn - 1, 0, 0).wait_recv()
            share(turn - 1, 0, 2).start()

            @pl.when(has_from)
            def _():
                relay(turn - 1).wait_recv()
                share(turn - 1, 1, 0).start()
                share(turn - 1, 1, 1).start()

        if turn - 2 in chunks:

            @pl.when(has_from)
            def _():
                share(turn - 2, 1, 0).wait_recv()
                share(turn - 2, 1, 2).start()

    for c in chunks:
        for kind in (1, 2):
            share(c, 0, kind).wait_recv()

    @pl.when(has_from)
    def _():
        for c in chunks:
            for kind in (1, 2):
                share(c, 1, kind).wait_recv()

    for k in range(3):
        for copy in to_mate(k):
            copy.wait_recv()
    for c in chunks:
        first(c).wait_send()
        for kind in range(3):
            share(c, 0, kind).wait_send()

    @pl.when(has_to)
    def _():
        for c in chunks:
            relay(c).wait_send()

    @pl.when(has_from)
    def _():
        for c in chunks:
            for kind in range(3):
                share(c, 1, kind).wait_send()

    for k in range(3):
        for copy in to_mate(k):
            copy.wait_send()


def shift_kernel(counts, steps, home, part_ref, out_ref, *rest):
    home_ref = rest[0] if home else None
    send_sem, recv_sem = rest[-2:]
    n_sec, blocks = counts
    sec, blk = lax.axis_index("sec"), lax.axis_index("blk")
    to, source = sec + steps, sec - steps
    has_to = jnp.logical_and(to >= 0, to < n_sec)
    has_from = jnp.logical_and(source >= 0, source < n_sec)
    targets = [(blk + turn) % blocks for turn in range(blocks)]
    mates = [(sec >= 0, sec, mate) for mate in targets[1:]] if home else []
    greet(mates + [(has_to, to, mate) for mate in targets] + [(has_from, source, mate) for mate in targets])

    def copy(turn):
        return send(part_ref, out_ref.at[blk], (send_sem, recv_sem), turn, to, targets[turn])

    def homeward(turn, owner):
        src = part_ref.at[targets[turn]]
        return send(src, home_ref.at[owner], (send_sem, recv_sem), blocks + turn - 1, sec, targets[turn])

    def arrival(turn):
        slot = out_ref.at[(blk + blocks - turn) % blocks]
        return send(part_ref, slot, (send_sem, recv_sem), turn, to, targets[turn])

    @pl.when(has_to)
    def _():
        for turn in range(blocks):
            copy(turn).start()

    if home:
        for turn in range(1, blocks):
            homeward(turn, blk).start()
        home_ref[blk] = part_ref[blk]
        for turn in range(1, blocks):
            homeward(turn, (blk + blocks - turn) % blocks).wait_recv()

    @pl.when(has_from)
    def _():
        for turn in range(blocks):
            arrival(turn).wait_recv()

    @pl.when(jnp.logical_not(has_from))
    def _():
        out_ref[...] = jnp.zeros_like(out_ref)

    @pl.when(has_to)
    def _():
        for turn in range(blocks):
            copy(turn).wait_send()

    if home:
        for turn in range(1, blocks):
            homeward(turn, blk).wait_send()


def return_kernel(counts, smooth_ref, out_ref, send_sem, recv_sem):
    n_sec, blocks = counts
    sec, blk = lax.axis_index("sec"), lax.axis_index("blk")
    held_blk, width = smooth_ref.shape[1], smooth_ref.shape[3]
    mates = [(blk + turn) % blocks for turn in range(blocks)]
    greet([(sec >= 0, sec, mate) for mate in mates[1:]])

    def copies(turn, owner):
        found = []
        for place in range(held_blk):
            start = pl.multiple_of(lane_of(owner, place, blocks), width)
            src, dst = smooth_ref.at[mates[turn], place], out_ref.at[:, pl.ds(start, width)]
            found.append(send(src, dst, (send_sem, recv_sem), held_blk * (turn - 1) + place, sec, mates[turn]))
        return found

    for turn in range(1, blocks):
        for copy in copies(turn, blk):
            copy.start()
    for place in range(held_blk):
        start = pl.multiple_of(lane_of(blk, place, blocks), width)
        out_ref[:, pl.ds(start, width)] = smooth_ref[blk, place]
    for turn in range(1, blocks):
        for copy in copies(turn, (blk + blocks - turn) % blocks):
            copy.wait_recv()
    for turn in range(1, blocks):
        for copy in copies(turn, blk):
            copy.wait_send()


def in_vmem(count):
    return [pl.BlockSpec(memory_space=pltpu.VMEM)] * count


def exchange(kernel, number, out_shape, operands, scratch):
    outs = jax.tree.map(lambda _: pl.BlockSpec(memory_space=pltpu.VMEM), out_shape)
    return pl.pallas_call(
        kernel, out_shape=out_shape, in_specs=in_vmem(len(operands)), out_specs=outs, scratch_shapes=scratch,
        compiler_params=pltpu.CompilerParams(collective_id=number, has_side_effects=True),
    )(*operands)


def call(kernel, out_shape, operands, scratch):
    outs = jax.tree.map(lambda _: pl.BlockSpec(memory_space=pltpu.VMEM), out_shape)
    return pl.pallas_call(
        kernel, out_shape=out_shape,
        in_specs=[pl.BlockSpec(memory_space=pltpu.SMEM)] + in_vmem(len(operands) - 1),
        out_specs=outs, scratch_shapes=scratch,
    )(*operands)


def body(features, programs, column_pot, tile_pairs, pair_counts):
    feat, cells_blk = features.shape[1:]
    progs = programs.shape[1]
    tiles_blk = cells_blk // TILE
    most = tile_pairs.shape[2]
    blocks, n_sec = lax.axis_size("blk"), lax.axis_size("sec")
    tiles = tiles_blk * blocks
    width = TILE // SPLITS
    held_blk = tiles_blk * SPLITS // blocks
    held = blocks * held_blk
    dims = (feat, blocks, tiles_blk, most)
    counts = (n_sec, blocks)
    f32, bf16 = jnp.float32, jnp.bfloat16
    shape = jax.ShapeDtypeStruct
    long = -(-(2 * most + 1) // 128) * 128
    listed = jnp.concatenate([tile_pairs[0], tile_pairs[1], pair_counts], axis=1)
    listed = jnp.pad(listed, ((0, 0), (0, long - listed.shape[1])))
    dma = pltpu.SemaphoreType.DMA
    mate_copies = (blocks - 1) * (held_blk + 2)

    own, xs, progs_all, pot, lists_all, lists = exchange(
        functools.partial(gather_kernel, counts), 0,
        (
            shape((blocks, held_blk, feat, width), bf16),
            shape((2, blocks, feat, cells_blk), bf16),
            shape((2, blocks, progs, cells_blk), bf16),
            shape((blocks, 1, cells_blk), bf16),
            shape((2, blocks, 1, long), jnp.int32),
            shape((blocks, 1, long), jnp.int32),
        ),
        (features[0], programs[0], column_pot, listed),
        [dma((STAGES * 5,)), dma((STAGES * 5,)), dma((mate_copies,)), dma((mate_copies,))],
    )

    xrec = pltpu.VMEM((held, 2 * HALF, width), bf16)
    yrec = pltpu.VMEM(((tiles + 1) * TILE, 2 * HALF), bf16)
    build = pltpu.VMEM((2 * HALF, TILE), f32)
    ext = pltpu.VMEM((tiles + 1, EXT, TILE), bf16)
    stat = pltpu.VMEM((held, 1, width), f32)
    acc = pltpu.VMEM((held, EXT, width), f32)
    index = pltpu.SMEM((blocks * most + 2 * UNROLL,), jnp.int32)
    ready = [pltpu.VMEM((TILE, width), f32)] * UNROLL
    tops = pltpu.VMEM((UNROLL, 1, width), f32)
    pots = shape((blocks, held_blk, width), f32)
    all_pots = shape((blocks, blocks, held_blk, width), f32)
    sums = shape((held, EXT, width), f32)

    row_own = call(
        functools.partial(row_kernel, dims), pots, (lists, own, xs, pot),
        [xrec, yrec, build, stat, stat, index, index, *ready],
    )
    row_prev, row_home = exchange(
        functools.partial(shift_kernel, counts, 1, True), 1, (all_pots, pots), (row_own,),
        [dma((2 * blocks - 1,)), dma((2 * blocks - 1,))],
    )
    col_own, back = call(
        functools.partial(col_kernel, dims), (pots, sums), (lists_all, own, xs, row_prev, progs_all),
        [xrec, yrec, build, ext, stat, stat, acc, index, index, tops, *ready],
    )
    col_all = exchange(
        functools.partial(shift_kernel, counts, -1, False), 2, all_pots, (col_own,), [dma((blocks,)), dma((blocks,))]
    )
    line = shape((1, cells_blk), f32)
    smooth, row_out, col_out = call(
        functools.partial(plan_kernel, dims),
        (shape((blocks, held_blk, progs, width), bf16), line, line),
        (lists, own, xs, row_own, col_all, progs_all, back, row_home),
        [xrec, yrec, build, ext, acc, index, index, *ready],
    )
    return_copies = (blocks - 1) * held_blk
    smoothed = exchange(
        functools.partial(return_kernel, counts), 3, shape((progs, cells_blk), bf16), (smooth,),
        [dma((return_copies,)), dma((return_copies,))],
    )
    return smoothed[None], row_out, col_out


def solution(mesh):
    in_specs = (
        P("sec", None, "blk"),
        P("sec", None, "blk"),
        P("sec", "blk"),
        P(None, "sec", "blk"),
        P("sec", "blk"),
    )
    out_specs = (P("sec", None, "blk"), P("sec", "blk"), P("sec", "blk"))
    return jax.shard_map(body, mesh=mesh, in_specs=in_specs, out_specs=out_specs, check_vma=False)
```

```python
import functools
import math

import jax
import jax.numpy as jnp
from jax import lax
from jax.experimental import pallas as pl
from jax.experimental.pallas import tpu as pltpu
from jax.sharding import PartitionSpec as P

TILE = 512
EPSILON = 0.05
LOG2E = math.log2(math.e)
LN2 = math.log(2.0)
NEG = -1e30
UNROLL = 2
SPLITS = 2
HALF = 64
EXT = 48


def split3(value):
    hi = value.astype(jnp.bfloat16).astype(jnp.float32)
    rest = value - hi
    mid = rest.astype(jnp.bfloat16).astype(jnp.float32)
    return hi, mid, rest - mid


def rows_of(pieces, width):
    index = lax.broadcasted_iota(jnp.int32, (8, width), 0)
    block = jnp.zeros((8, width), jnp.float32)
    for place, piece in enumerate(pieces):
        block = jnp.where(index == place, piece, block)
    return block


def sum_squares(cells):
    return jnp.sum(cells * cells, axis=0, keepdims=True)


def own_records(own_ref, xrec, feat, tiles_blk, tiles, bias_of):
    width = TILE // SPLITS
    gain = 2.0 * LOG2E / (feat * EPSILON)
    xrec[...] = jnp.zeros_like(xrec)

    def one(tile, carry):
        cells = own_ref[tile // tiles_blk, tile % tiles_blk].astype(jnp.float32)
        scaled = cells * gain
        high = scaled.astype(jnp.bfloat16)
        xrec[tile, 0:feat, :] = high
        xrec[tile, HALF : HALF + feat, :] = (scaled - high.astype(jnp.float32)).astype(jnp.bfloat16)
        bias = split3(bias_of(tile, cells))
        ones = jnp.ones((1, width), jnp.float32)
        aux = rows_of((ones, ones, ones) + bias, width)
        xrec[tile, HALF - 8 : HALF, :] = aux.astype(jnp.bfloat16)
        return carry

    lax.fori_loop(0, tiles, one, 0)


def other_records(other_ref, yrec, build, feat, tiles_blk, tiles, bias_of):
    build[...] = jnp.zeros_like(build)
    ones = jnp.ones((1, TILE), jnp.float32)

    def one(block, carry):
        for step in range(tiles_blk):
            tile, start, part = block * tiles_blk + step, step * TILE, build.at[step]
            cells = other_ref[block, 0:feat, start : start + TILE].astype(jnp.float32)
            part[0:feat, :] = cells
            part[HALF : HALF + feat, :] = cells
            bias = split3(bias_of(tile, start, cells))
            part[HALF - 8 : HALF, :] = rows_of(bias + (ones, ones, ones), TILE)
        for step in range(tiles_blk):
            tile = block * tiles_blk + step
            yrec[pl.ds(pl.multiple_of(tile * TILE, TILE), TILE), :] = build[step].T.astype(jnp.bfloat16)
        return carry

    lax.fori_loop(0, tiles // tiles_blk, one, 0)
    lane = lax.broadcasted_iota(jnp.int32, (TILE, 2 * HALF), 1)
    yrec[tiles * TILE : (tiles + 1) * TILE, :] = jnp.where(lane == HALF - 8, NEG, 0.0).astype(
        jnp.bfloat16
    )


def ext_records(prog_ref, ext, progs, tiles_blk, tiles):
    index = lax.broadcasted_iota(jnp.int32, (EXT - progs, TILE), 0)
    tail = jnp.where(index == 0, 1.0, 0.0).astype(jnp.bfloat16)

    def one(tile, carry):
        start = pl.multiple_of((tile % tiles_blk) * TILE, TILE)
        ext[tile, 0:progs, :] = prog_ref[tile // tiles_blk, :, pl.ds(start, TILE)]
        ext[tile, progs:EXT, :] = tail
        return carry

    lax.fori_loop(0, tiles, one, 0)
    ext[tiles] = jnp.zeros((EXT, TILE), jnp.bfloat16)


def listed_pairs(lists_ref, mine, other, most, blocks, tiles_blk, tiles, own_first, used=True):
    kinds = blocks // SPLITS
    kind = lax.axis_index("blk") // SPLITS

    def of_block(block, place):
        def one(slot, at):
            row = lists_ref[block, 0, slot] + block * tiles_blk
            col = lists_ref[block, 0, most + slot]
            held, across = (row, col) if own_first else (col, row)
            mine[at] = held // kinds
            other[at] = across
            return at + jnp.where(held % kinds == kind, 1, 0)

        return lax.fori_loop(0, jnp.where(used, lists_ref[block, 0, 2 * most], 0), one, place)

    total = lax.fori_loop(0, blocks, of_block, 0)
    last = jnp.where(total > 0, mine[jnp.maximum(total - 1, 0)], 0)
    for extra in range(2 * UNROLL):
        mine[total + extra] = last
        other[total + extra] = tiles
    return (total + UNROLL - 1) // UNROLL


def scores_of(yrec, xrec, mine, other):
    rows = yrec[pl.ds(pl.multiple_of(other * TILE, TILE), TILE), :]
    return jnp.dot(rows, xrec[mine], preferred_element_type=jnp.float32)


def over_pairs(groups, ready, tops, yrec, xrec, mine, other, use):
    def make(at, place):
        scores = scores_of(yrec, xrec, mine[at], other[at])
        ready[place][...] = scores
        if tops is not None:
            tops[place] = jnp.max(scores, axis=0, keepdims=True)

    make(0, 0)

    def group(index, carry):
        for step in range(UNROLL):
            at = index * UNROLL + step
            make(at + 1, (step + 1) % UNROLL)
            use(ready[step], None if tops is None else tops[step], mine[at], other[at])
        return carry

    lax.fori_loop(0, groups, group, 0)


def spread(parts_ref, tile, blocks, tiles_blk):
    kinds = blocks // SPLITS
    first = (tile % kinds) * SPLITS
    place = (tile % tiles_blk) // kinds
    parts = [parts_ref[first + n, tile // tiles_blk, pl.ds(place, 1), :] for n in range(SPLITS)]
    return jnp.concatenate(parts, axis=1)


def near_side(forward):
    odd = lax.axis_index("sec") % 2
    return odd if forward else 1 - odd


def lane_of(owner, place, blocks):
    kinds = blocks // SPLITS
    return (place * kinds + owner // SPLITS) * TILE + (owner % SPLITS) * (TILE // SPLITS)


def row_kernel(dims, lists_ref, own_ref, next_ref, pot_ref, rp_ref, xrec, yrec, build, high, total, mine, other, *ready):
    feat, blocks, tiles_blk, most = dims
    tiles = blocks * tiles_blk
    held_blk = tiles_blk * SPLITS // blocks
    held = blocks * held_blk
    to_score = LOG2E / EPSILON
    groups = listed_pairs(lists_ref, mine, other, most, blocks, tiles_blk, tiles, True)
    own_records(
        own_ref, xrec, feat, held_blk, held,
        lambda tile, cells: jnp.zeros((1, cells.shape[1]), jnp.float32),
    )

    def bias(tile, start, cells):
        pot = pot_ref[tile // tiles_blk, :, pl.ds(start, TILE)].astype(jnp.float32)
        return (pot - sum_squares(cells) / feat) * to_score

    other_records(next_ref.at[near_side(True)], yrec, build, feat, tiles_blk, tiles, bias)
    high[...] = jnp.full_like(high, NEG)
    total[...] = jnp.zeros_like(total)

    def use(scores_ref, top, row, col):
        old = high[row]
        new = jnp.maximum(old, jnp.max(scores_ref[...], axis=0, keepdims=True))
        part = jnp.sum(jnp.exp2(scores_ref[...] - new), axis=0, keepdims=True)
        total[row] = total[row] * jnp.exp2(old - new) + part
        high[row] = new

    over_pairs(groups, ready, None, yrec, xrec, mine, other, use)
    at_end = lax.axis_index("sec") == lax.axis_size("sec") - 1
    for tile in range(held):
        cells = own_ref[tile // held_blk, tile % held_blk].astype(jnp.float32)
        score = high[tile] + jnp.log2(total[tile]) - sum_squares(cells) * (to_score / feat)
        rp_ref[tile // held_blk, tile % held_blk : tile % held_blk + 1, :] = jnp.where(at_end, 0.0, score * (-EPSILON * LN2))


def col_kernel(dims, lists_ref, own_ref, prev_ref, rp_ref, prog_ref, cp_ref, back_ref,
               xrec, yrec, build, ext, high, total, acc, mine, other, tops, *ready):
    feat, blocks, tiles_blk, most = dims
    tiles = blocks * tiles_blk
    held_blk = tiles_blk * SPLITS // blocks
    held = blocks * held_blk
    to_score = LOG2E / EPSILON
    progs = prog_ref.shape[2]
    used = lax.axis_index("sec") > 0
    groups = listed_pairs(
        lists_ref.at[near_side(False)], mine, other, most, blocks, tiles_blk, tiles, False, used
    )
    own_records(
        own_ref, xrec, feat, held_blk, held,
        lambda tile, cells: jnp.zeros((1, cells.shape[1]), jnp.float32),
    )

    def bias(tile, start, cells):
        return (spread(rp_ref, tile, blocks, tiles_blk) - sum_squares(cells) / feat) * to_score

    other_records(prev_ref.at[near_side(False)], yrec, build, feat, tiles_blk, tiles, bias)
    ext_records(prog_ref.at[near_side(False)], ext, progs, tiles_blk, tiles)
    high[...] = jnp.full_like(high, NEG)
    total[...] = jnp.zeros_like(total)
    acc[...] = jnp.zeros_like(acc)

    def use(scores_ref, top, col, row):
        old = high[col]
        new = jnp.maximum(old, top)
        weight = jnp.exp2(scores_ref[...] - new)
        part = jnp.sum(weight, axis=0, keepdims=True)
        shrink = jnp.exp2(old - new)
        sums = jnp.dot(ext[row], weight.astype(jnp.bfloat16), preferred_element_type=jnp.float32)
        acc[col] = acc[col] * shrink + sums
        total[col] = total[col] * shrink + part
        high[col] = new

    over_pairs(groups, ready, tops, yrec, xrec, mine, other, use)
    for tile in range(held):
        cells = own_ref[tile // held_blk, tile % held_blk].astype(jnp.float32)
        filled = total[tile] > 0.0
        score = high[tile] + jnp.log2(total[tile]) - sum_squares(cells) * (to_score / feat)
        cp_ref[tile // held_blk, tile % held_blk : tile % held_blk + 1, :] = jnp.where(filled, score * (-EPSILON * LN2), 0.0)
        back_ref[tile] = jnp.where(filled, acc[tile] / total[tile], 0.0)


def plan_kernel(dims, lists_ref, own_ref, next_ref, rp_ref, cp_ref, prog_ref, back_ref, home_ref, out_ref, rows_ref, cols_ref,
                xrec, yrec, build, ext, acc, mine, other, *ready):
    feat, blocks, tiles_blk, most = dims
    tiles = blocks * tiles_blk
    held_blk = tiles_blk * SPLITS // blocks
    held = blocks * held_blk
    to_score = LOG2E / EPSILON
    progs = prog_ref.shape[2]
    groups = listed_pairs(lists_ref, mine, other, most, blocks, tiles_blk, tiles, True)
    own_records(
        own_ref, xrec, feat, held_blk, held,
        lambda tile, cells: (rp_ref[tile // held_blk, pl.ds(tile % held_blk, 1), :] - sum_squares(cells) / feat) * to_score,
    )

    def bias(tile, start, cells):
        return (spread(cp_ref, tile, blocks, tiles_blk) - sum_squares(cells) / feat) * to_score

    other_records(next_ref.at[near_side(True)], yrec, build, feat, tiles_blk, tiles, bias)
    ext_records(prog_ref.at[near_side(True)], ext, progs, tiles_blk, tiles)
    acc[...] = back_ref[...]
    width = TILE // SPLITS
    for owner in range(blocks):
        for place in range(held_blk):
            start = lane_of(owner, place, blocks)
            rows_ref[:, start : start + width] = home_ref[owner, place : place + 1, :]
            cols_ref[:, start : start + width] = cp_ref[owner, lax.axis_index("blk"), place : place + 1, :]

    def use(scores_ref, top, row, col):
        plan = jnp.exp2(scores_ref[...]).astype(jnp.bfloat16)
        acc[row] = acc[row] + jnp.dot(ext[col], plan, preferred_element_type=jnp.float32)

    over_pairs(groups, ready, None, yrec, xrec, mine, other, use)
    for tile in range(held):
        sums = acc[tile]
        out_ref[tile // held_blk, tile % held_blk] = (sums[0:progs] / sums[progs : progs + 1]).astype(jnp.bfloat16)


MESH = pl.DeviceIdType.MESH


def greet(targets):
    barrier = pltpu.get_barrier_semaphore()
    expected = jnp.int32(0)
    for used, sec, blk in targets:

        @pl.when(used)
        def _():
            pl.semaphore_signal(barrier, inc=1, device_id=(sec, blk), device_id_type=MESH)

        expected = expected + jnp.where(used, 1, 0)
    pl.semaphore_wait(barrier, expected)


def send(src, dst, sems, place, sec, blk):
    return pltpu.make_async_remote_copy(
        src_ref=src, dst_ref=dst, send_sem=sems[0].at[place], recv_sem=sems[1].at[place],
        device_id=(sec, blk), device_id_type=MESH,
    )


STAGES = 8


def gather_kernel(counts, x_ref, prog_ref, pot_ref, list_ref, own_ref, xs_ref, progs_ref, pots_ref, lists_ref,
                  all_lists_ref, send_sem, recv_sem, mate_send, mate_recv):
    n_sec, blocks = counts
    sec, blk = lax.axis_index("sec"), lax.axis_index("blk")
    even = sec % 2 == 0
    partner = jnp.where(even, sec + 1, sec - 1)
    relay_to = jnp.where(even, sec + 2, sec - 2)
    relay_from = jnp.where(even, sec - 2, sec + 2)
    has_to = jnp.logical_and(relay_to >= 0, relay_to < n_sec)
    has_from = jnp.logical_and(relay_from >= 0, relay_from < n_sec)
    core = blk + 1 - 2 * (blk % 2)
    across = (blk + 2) % blocks
    corner = core + 2 - 4 * (core // 2)
    mates = (core, across, corner)
    yes = sec >= 0
    greet(
        [(yes, partner, blk), (has_to, relay_to, blk), (has_from, relay_from, blk)]
        + [(yes, sec, mate) for mate in mates]
    )
    sems, mate_sems = (send_sem, recv_sem), (mate_send, mate_recv)
    width = TILE // SPLITS
    held_blk = x_ref.shape[1] // TILE * SPLITS // blocks
    half = x_ref.shape[1] // 2
    sources = [
        (list_ref, lists_ref, None), (x_ref, xs_ref, 0), (x_ref, xs_ref, 1), (prog_ref, progs_ref, 0), (prog_ref, progs_ref, 1),
    ]

    def cut(ref, part):
        return ref if part is None else ref.at[:, part * half : (part + 1) * half]

    def place_of(buffer, side, owner, part):
        return cut(buffer.at[side, owner], part)

    def first(c):
        src, buffer, part = sources[c]
        return send(cut(src, part), place_of(buffer, 0, blk, part), sems, STAGES * c, partner, blk)

    def relay(c):
        _, buffer, part = sources[c]
        return send(
            place_of(buffer, 0, blk, part), place_of(buffer, 1, blk, part), sems, STAGES * c + 1, relay_to, blk
        )

    def share(c, side, kind):
        _, buffer, part = sources[c]
        owner = across if kind == 2 else blk
        slot = place_of(buffer, side, owner, part)
        return send(slot, slot, sems, STAGES * c + 2 + 3 * side + kind, sec, across if kind == 0 else core)

    def to_mate(k):
        mate = mates[k]
        copies = []
        for tile in range(held_blk):
            start = pl.multiple_of(lane_of(mate, tile, blocks), width)
            copies.append((x_ref.at[:, pl.ds(start, width)], own_ref.at[blk, tile]))
        copies.append((pot_ref, pots_ref.at[blk]))
        copies.append((list_ref, all_lists_ref.at[blk]))
        per = len(copies)
        return [send(src, dst, mate_sems, per * k + n, sec, mate) for n, (src, dst) in enumerate(copies)]

    chunks = range(len(sources))
    for c in chunks:
        first(c).start()
    for k in range(3):
        for copy in to_mate(k):
            copy.start()
    for tile in range(held_blk):
        start = pl.multiple_of(lane_of(blk, tile, blocks), width)
        own_ref[blk, tile] = x_ref[:, pl.ds(start, width)]
    pots_ref[blk] = pot_ref[...]
    all_lists_ref[blk] = list_ref[...]
    for turn in range(len(sources) + 2):
        if turn in chunks:
            first(turn).wait_recv()

            @pl.when(has_to)
            def _():
                relay(turn).start()

            share(turn, 0, 0).start()
            share(turn, 0, 1).start()
        if turn - 1 in chunks:
            share(turn - 1, 0, 0).wait_recv()
            share(turn - 1, 0, 2).start()

            @pl.when(has_from)
            def _():
                relay(turn - 1).wait_recv()
                share(turn - 1, 1, 0).start()
                share(turn - 1, 1, 1).start()

        if turn - 2 in chunks:

            @pl.when(has_from)
            def _():
                share(turn - 2, 1, 0).wait_recv()
                share(turn - 2, 1, 2).start()

    for c in chunks:
        for kind in (1, 2):
            share(c, 0, kind).wait_recv()

    @pl.when(has_from)
    def _():
        for c in chunks:
            for kind in (1, 2):
                share(c, 1, kind).wait_recv()

    for k in range(3):
        for copy in to_mate(k):
            copy.wait_recv()
    for c in chunks:
        first(c).wait_send()
        for kind in range(3):
            share(c, 0, kind).wait_send()

    @pl.when(has_to)
    def _():
        for c in chunks:
            relay(c).wait_send()

    @pl.when(has_from)
    def _():
        for c in chunks:
            for kind in range(3):
                share(c, 1, kind).wait_send()

    for k in range(3):
        for copy in to_mate(k):
            copy.wait_send()


def shift_kernel(counts, steps, home, part_ref, out_ref, *rest):
    home_ref = rest[0] if home else None
    send_sem, recv_sem = rest[-2:]
    n_sec, blocks = counts
    sec, blk = lax.axis_index("sec"), lax.axis_index("blk")
    to, source = sec + steps, sec - steps
    has_to = jnp.logical_and(to >= 0, to < n_sec)
    has_from = jnp.logical_and(source >= 0, source < n_sec)
    targets = [(blk + turn) % blocks for turn in range(blocks)]
    mates = [(sec >= 0, sec, mate) for mate in targets[1:]] if home else []
    greet(mates + [(has_to, to, mate) for mate in targets] + [(has_from, source, mate) for mate in targets])

    def copy(turn):
        return send(part_ref, out_ref.at[blk], (send_sem, recv_sem), turn, to, targets[turn])

    def homeward(turn, owner):
        src = part_ref.at[targets[turn]]
        return send(src, home_ref.at[owner], (send_sem, recv_sem), blocks + turn - 1, sec, targets[turn])

    def arrival(turn):
        slot = out_ref.at[(blk + blocks - turn) % blocks]
        return send(part_ref, slot, (send_sem, recv_sem), turn, to, targets[turn])

    @pl.when(has_to)
    def _():
        for turn in range(blocks):
            copy(turn).start()

    if home:
        for turn in range(1, blocks):
            homeward(turn, blk).start()
        home_ref[blk] = part_ref[blk]
        for turn in range(1, blocks):
            homeward(turn, (blk + blocks - turn) % blocks).wait_recv()

    @pl.when(has_from)
    def _():
        for turn in range(blocks):
            arrival(turn).wait_recv()

    @pl.when(jnp.logical_not(has_from))
    def _():
        out_ref[...] = jnp.zeros_like(out_ref)

    @pl.when(has_to)
    def _():
        for turn in range(blocks):
            copy(turn).wait_send()

    if home:
        for turn in range(1, blocks):
            homeward(turn, blk).wait_send()


def return_kernel(counts, smooth_ref, out_ref, send_sem, recv_sem):
    n_sec, blocks = counts
    sec, blk = lax.axis_index("sec"), lax.axis_index("blk")
    held_blk, width = smooth_ref.shape[1], smooth_ref.shape[3]
    mates = [(blk + turn) % blocks for turn in range(blocks)]
    greet([(sec >= 0, sec, mate) for mate in mates[1:]])

    def copies(turn, owner):
        found = []
        for place in range(held_blk):
            start = pl.multiple_of(lane_of(owner, place, blocks), width)
            src, dst = smooth_ref.at[mates[turn], place], out_ref.at[:, pl.ds(start, width)]
            found.append(send(src, dst, (send_sem, recv_sem), held_blk * (turn - 1) + place, sec, mates[turn]))
        return found

    for turn in range(1, blocks):
        for copy in copies(turn, blk):
            copy.start()
    for place in range(held_blk):
        start = pl.multiple_of(lane_of(blk, place, blocks), width)
        out_ref[:, pl.ds(start, width)] = smooth_ref[blk, place]
    for turn in range(1, blocks):
        for copy in copies(turn, (blk + blocks - turn) % blocks):
            copy.wait_recv()
    for turn in range(1, blocks):
        for copy in copies(turn, blk):
            copy.wait_send()


def in_vmem(count):
    return [pl.BlockSpec(memory_space=pltpu.VMEM)] * count


def exchange(kernel, number, out_shape, operands, scratch):
    outs = jax.tree.map(lambda _: pl.BlockSpec(memory_space=pltpu.VMEM), out_shape)
    return pl.pallas_call(
        kernel, out_shape=out_shape, in_specs=in_vmem(len(operands)), out_specs=outs, scratch_shapes=scratch,
        compiler_params=pltpu.CompilerParams(collective_id=number, has_side_effects=True),
    )(*operands)


def call(kernel, out_shape, operands, scratch):
    outs = jax.tree.map(lambda _: pl.BlockSpec(memory_space=pltpu.VMEM), out_shape)
    return pl.pallas_call(
        kernel, out_shape=out_shape,
        in_specs=[pl.BlockSpec(memory_space=pltpu.SMEM)] + in_vmem(len(operands) - 1),
        out_specs=outs, scratch_shapes=scratch,
    )(*operands)


def body(features, programs, column_pot, tile_pairs, pair_counts):
    feat, cells_blk = features.shape[1:]
    progs = programs.shape[1]
    tiles_blk = cells_blk // TILE
    most = tile_pairs.shape[2]
    blocks, n_sec = lax.axis_size("blk"), lax.axis_size("sec")
    tiles = tiles_blk * blocks
    width = TILE // SPLITS
    held_blk = tiles_blk * SPLITS // blocks
    held = blocks * held_blk
    dims = (feat, blocks, tiles_blk, most)
    counts = (n_sec, blocks)
    f32, bf16 = jnp.float32, jnp.bfloat16
    shape = jax.ShapeDtypeStruct
    long = -(-(2 * most + 1) // 128) * 128
    listed = jnp.concatenate([tile_pairs[0], tile_pairs[1], pair_counts], axis=1)
    listed = jnp.pad(listed, ((0, 0), (0, long - listed.shape[1])))
    dma = pltpu.SemaphoreType.DMA
    mate_copies = (blocks - 1) * (held_blk + 2)

    own, xs, progs_all, pot, lists_all, lists = exchange(
        functools.partial(gather_kernel, counts), 0,
        (
            shape((blocks, held_blk, feat, width), bf16),
            shape((2, blocks, feat, cells_blk), bf16),
            shape((2, blocks, progs, cells_blk), bf16),
            shape((blocks, 1, cells_blk), bf16),
            shape((2, blocks, 1, long), jnp.int32),
            shape((blocks, 1, long), jnp.int32),
        ),
        (features[0], programs[0], column_pot, listed),
        [dma((STAGES * 5,)), dma((STAGES * 5,)), dma((mate_copies,)), dma((mate_copies,))],
    )

    xrec = pltpu.VMEM((held, 2 * HALF, width), bf16)
    yrec = pltpu.VMEM(((tiles + 1) * TILE, 2 * HALF), bf16)
    build = pltpu.VMEM((tiles_blk, 2 * HALF, TILE), f32)
    ext = pltpu.VMEM((tiles + 1, EXT, TILE), bf16)
    stat = pltpu.VMEM((held, 1, width), f32)
    acc = pltpu.VMEM((held, EXT, width), f32)
    index = pltpu.SMEM((blocks * most + 2 * UNROLL,), jnp.int32)
    ready = [pltpu.VMEM((TILE, width), f32)] * UNROLL
    tops = pltpu.VMEM((UNROLL, 1, width), f32)
    pots = shape((blocks, held_blk, width), f32)
    all_pots = shape((blocks, blocks, held_blk, width), f32)
    sums = shape((held, EXT, width), f32)

    row_own = call(
        functools.partial(row_kernel, dims), pots, (lists, own, xs, pot),
        [xrec, yrec, build, stat, stat, index, index, *ready],
    )
    row_prev, row_home = exchange(
        functools.partial(shift_kernel, counts, 1, True), 1, (all_pots, pots), (row_own,),
        [dma((2 * blocks - 1,)), dma((2 * blocks - 1,))],
    )
    col_own, back = call(
        functools.partial(col_kernel, dims), (pots, sums), (lists_all, own, xs, row_prev, progs_all),
        [xrec, yrec, build, ext, stat, stat, acc, index, index, tops, *ready],
    )
    col_all = exchange(
        functools.partial(shift_kernel, counts, -1, False), 2, all_pots, (col_own,), [dma((blocks,)), dma((blocks,))]
    )
    line = shape((1, cells_blk), f32)
    smooth, row_out, col_out = call(
        functools.partial(plan_kernel, dims),
        (shape((blocks, held_blk, progs, width), bf16), line, line),
        (lists, own, xs, row_own, col_all, progs_all, back, row_home),
        [xrec, yrec, build, ext, acc, index, index, *ready],
    )
    return_copies = (blocks - 1) * held_blk
    smoothed = exchange(
        functools.partial(return_kernel, counts), 3, shape((progs, cells_blk), bf16), (smooth,),
        [dma((return_copies,)), dma((return_copies,))],
    )
    return smoothed[None], row_out, col_out


def solution(mesh):
    in_specs = (
        P("sec", None, "blk"),
        P("sec", None, "blk"),
        P("sec", "blk"),
        P(None, "sec", "blk"),
        P("sec", "blk"),
    )
    out_specs = (P("sec", None, "blk"), P("sec", "blk"), P("sec", "blk"))
    return jax.shard_map(body, mesh=mesh, in_specs=in_specs, out_specs=out_specs, check_vma=False)
```

```python
import functools
import math

import jax
import jax.numpy as jnp
from jax import lax
from jax.experimental import pallas as pl
from jax.experimental.pallas import tpu as pltpu
from jax.sharding import PartitionSpec as P

TILE = 512
EPSILON = 0.05
LOG2E = math.log2(math.e)
LN2 = math.log(2.0)
NEG = -1e30
UNROLL = 2
SPLITS = 2
HALF = 64
EXT = 48


def split3(value):
    hi = value.astype(jnp.bfloat16).astype(jnp.float32)
    rest = value - hi
    mid = rest.astype(jnp.bfloat16).astype(jnp.float32)
    return hi, mid, rest - mid


def rows_of(pieces, width):
    index = lax.broadcasted_iota(jnp.int32, (8, width), 0)
    block = jnp.zeros((8, width), jnp.float32)
    for place, piece in enumerate(pieces):
        block = jnp.where(index == place, piece, block)
    return block


def sum_squares(cells):
    return jnp.sum(cells * cells, axis=0, keepdims=True)


def own_records(own_ref, xrec, feat, tiles_blk, tiles, bias_of):
    width = TILE // SPLITS
    gain = 2.0 * LOG2E / (feat * EPSILON)
    xrec[...] = jnp.zeros_like(xrec)

    def one(tile, carry):
        cells = own_ref[tile // tiles_blk, tile % tiles_blk].astype(jnp.float32)
        scaled = cells * gain
        high = scaled.astype(jnp.bfloat16)
        xrec[tile, 0:feat, :] = high
        xrec[tile, HALF : HALF + feat, :] = (scaled - high.astype(jnp.float32)).astype(jnp.bfloat16)
        bias = split3(bias_of(tile, cells))
        ones = jnp.ones((1, width), jnp.float32)
        aux = rows_of((ones, ones, ones) + bias, width)
        xrec[tile, HALF - 8 : HALF, :] = aux.astype(jnp.bfloat16)
        return carry

    lax.fori_loop(0, tiles, one, 0, unroll=4)


def other_records(other_ref, yrec, build, feat, tiles_blk, tiles, bias_of):
    build[...] = jnp.zeros_like(build)
    ones = jnp.ones((1, TILE), jnp.float32)

    def one(block, carry):
        for step in range(tiles_blk):
            tile, start, part = block * tiles_blk + step, step * TILE, build.at[step]
            cells = other_ref[block, 0:feat, start : start + TILE].astype(jnp.float32)
            part[0:feat, :] = cells
            part[HALF : HALF + feat, :] = cells
            bias = split3(bias_of(tile, start, cells))
            part[HALF - 8 : HALF, :] = rows_of(bias + (ones, ones, ones), TILE)
        for step in range(tiles_blk):
            tile = block * tiles_blk + step
            yrec[pl.ds(pl.multiple_of(tile * TILE, TILE), TILE), :] = build[step].T.astype(jnp.bfloat16)
        return carry

    lax.fori_loop(0, tiles // tiles_blk, one, 0)
    lane = lax.broadcasted_iota(jnp.int32, (TILE, 2 * HALF), 1)
    yrec[tiles * TILE : (tiles + 1) * TILE, :] = jnp.where(lane == HALF - 8, NEG, 0.0).astype(
        jnp.bfloat16
    )


def ext_records(prog_ref, ext, progs, tiles_blk, tiles):
    index = lax.broadcasted_iota(jnp.int32, (EXT - progs, TILE), 0)
    tail = jnp.where(index == 0, 1.0, 0.0).astype(jnp.bfloat16)

    def one(tile, carry):
        start = pl.multiple_of((tile % tiles_blk) * TILE, TILE)
        ext[tile, 0:progs, :] = prog_ref[tile // tiles_blk, :, pl.ds(start, TILE)]
        ext[tile, progs:EXT, :] = tail
        return carry

    lax.fori_loop(0, tiles, one, 0, unroll=4)
    ext[tiles] = jnp.zeros((EXT, TILE), jnp.bfloat16)


def listed_pairs(lists_ref, mine, other, most, blocks, tiles_blk, tiles, own_first, used=True):
    kinds = blocks // SPLITS
    kind = lax.axis_index("blk") // SPLITS

    def of_block(block, place):
        def one(slot, at):
            row = lists_ref[block, 0, slot] + block * tiles_blk
            col = lists_ref[block, 0, most + slot]
            held, across = (row, col) if own_first else (col, row)
            mine[at] = held // kinds
            other[at] = across
            return at + jnp.where(held % kinds == kind, 1, 0)

        return lax.fori_loop(0, jnp.where(used, lists_ref[block, 0, 2 * most], 0), one, place)

    total = lax.fori_loop(0, blocks, of_block, 0)
    last = jnp.where(total > 0, mine[jnp.maximum(total - 1, 0)], 0)
    for extra in range(2 * UNROLL):
        mine[total + extra] = last
        other[total + extra] = tiles
    return (total + UNROLL - 1) // UNROLL


def scores_of(yrec, xrec, mine, other):
    rows = yrec[pl.ds(pl.multiple_of(other * TILE, TILE), TILE), :]
    return jnp.dot(rows, xrec[mine], preferred_element_type=jnp.float32)


def over_pairs(groups, ready, tops, yrec, xrec, mine, other, use):
    def make(at, place):
        scores = scores_of(yrec, xrec, mine[at], other[at])
        ready[place][...] = scores
        if tops is not None:
            tops[place] = jnp.max(scores, axis=0, keepdims=True)

    make(0, 0)

    def group(index, carry):
        for step in range(UNROLL):
            at = index * UNROLL + step
            make(at + 1, (step + 1) % UNROLL)
            use(ready[step], None if tops is None else tops[step], mine[at], other[at])
        return carry

    lax.fori_loop(0, groups, group, 0)


def spread(parts_ref, tile, blocks, tiles_blk):
    kinds = blocks // SPLITS
    first = (tile % kinds) * SPLITS
    place = (tile % tiles_blk) // kinds
    parts = [parts_ref[first + n, tile // tiles_blk, pl.ds(place, 1), :] for n in range(SPLITS)]
    return jnp.concatenate(parts, axis=1)


def near_side(forward):
    odd = lax.axis_index("sec") % 2
    return odd if forward else 1 - odd


def lane_of(owner, place, blocks):
    kinds = blocks // SPLITS
    return (place * kinds + owner // SPLITS) * TILE + (owner % SPLITS) * (TILE // SPLITS)


def row_kernel(dims, lists_ref, own_ref, next_ref, pot_ref, rp_ref, xrec, yrec, build, high, total, mine, other, *ready):
    feat, blocks, tiles_blk, most = dims
    tiles = blocks * tiles_blk
    held_blk = tiles_blk * SPLITS // blocks
    held = blocks * held_blk
    to_score = LOG2E / EPSILON
    groups = listed_pairs(lists_ref, mine, other, most, blocks, tiles_blk, tiles, True)
    own_records(
        own_ref, xrec, feat, held_blk, held,
        lambda tile, cells: jnp.zeros((1, cells.shape[1]), jnp.float32),
    )

    def bias(tile, start, cells):
        pot = pot_ref[tile // tiles_blk, :, pl.ds(start, TILE)].astype(jnp.float32)
        return (pot - sum_squares(cells) / feat) * to_score

    other_records(next_ref.at[near_side(True)], yrec, build, feat, tiles_blk, tiles, bias)
    high[...] = jnp.full_like(high, NEG)
    total[...] = jnp.zeros_like(total)

    def use(scores_ref, top, row, col):
        old = high[row]
        new = jnp.maximum(old, jnp.max(scores_ref[...], axis=0, keepdims=True))
        part = jnp.sum(jnp.exp2(scores_ref[...] - new), axis=0, keepdims=True)
        total[row] = total[row] * jnp.exp2(old - new) + part
        high[row] = new

    over_pairs(groups, ready, None, yrec, xrec, mine, other, use)
    at_end = lax.axis_index("sec") == lax.axis_size("sec") - 1
    for tile in range(held):
        cells = own_ref[tile // held_blk, tile % held_blk].astype(jnp.float32)
        score = high[tile] + jnp.log2(total[tile]) - sum_squares(cells) * (to_score / feat)
        rp_ref[tile // held_blk, tile % held_blk : tile % held_blk + 1, :] = jnp.where(at_end, 0.0, score * (-EPSILON * LN2))


def col_kernel(dims, lists_ref, own_ref, prev_ref, rp_ref, prog_ref, cp_ref, back_ref,
               xrec, yrec, build, ext, high, total, acc, mine, other, tops, *ready):
    feat, blocks, tiles_blk, most = dims
    tiles = blocks * tiles_blk
    held_blk = tiles_blk * SPLITS // blocks
    held = blocks * held_blk
    to_score = LOG2E / EPSILON
    progs = prog_ref.shape[2]
    used = lax.axis_index("sec") > 0
    groups = listed_pairs(
        lists_ref.at[near_side(False)], mine, other, most, blocks, tiles_blk, tiles, False, used
    )
    own_records(
        own_ref, xrec, feat, held_blk, held,
        lambda tile, cells: jnp.zeros((1, cells.shape[1]), jnp.float32),
    )

    def bias(tile, start, cells):
        return (spread(rp_ref, tile, blocks, tiles_blk) - sum_squares(cells) / feat) * to_score

    other_records(prev_ref.at[near_side(False)], yrec, build, feat, tiles_blk, tiles, bias)
    ext_records(prog_ref.at[near_side(False)], ext, progs, tiles_blk, tiles)
    high[...] = jnp.full_like(high, NEG)
    total[...] = jnp.zeros_like(total)
    acc[...] = jnp.zeros_like(acc)

    def use(scores_ref, top, col, row):
        old = high[col]
        new = jnp.maximum(old, top)
        weight = jnp.exp2(scores_ref[...] - new)
        part = jnp.sum(weight, axis=0, keepdims=True)
        shrink = jnp.exp2(old - new)
        sums = jnp.dot(ext[row], weight.astype(jnp.bfloat16), preferred_element_type=jnp.float32)
        acc[col] = acc[col] * shrink + sums
        total[col] = total[col] * shrink + part
        high[col] = new

    over_pairs(groups, ready, tops, yrec, xrec, mine, other, use)
    for tile in range(held):
        cells = own_ref[tile // held_blk, tile % held_blk].astype(jnp.float32)
        filled = total[tile] > 0.0
        score = high[tile] + jnp.log2(total[tile]) - sum_squares(cells) * (to_score / feat)
        cp_ref[tile // held_blk, tile % held_blk : tile % held_blk + 1, :] = jnp.where(filled, score * (-EPSILON * LN2), 0.0)
        back_ref[tile] = jnp.where(filled, acc[tile] / total[tile], 0.0)


def plan_kernel(dims, lists_ref, own_ref, next_ref, rp_ref, cp_ref, prog_ref, back_ref, home_ref, out_ref, rows_ref, cols_ref,
                xrec, yrec, build, ext, acc, mine, other, *ready):
    feat, blocks, tiles_blk, most = dims
    tiles = blocks * tiles_blk
    held_blk = tiles_blk * SPLITS // blocks
    held = blocks * held_blk
    to_score = LOG2E / EPSILON
    progs = prog_ref.shape[2]
    groups = listed_pairs(lists_ref, mine, other, most, blocks, tiles_blk, tiles, True)
    own_records(
        own_ref, xrec, feat, held_blk, held,
        lambda tile, cells: (rp_ref[tile // held_blk, pl.ds(tile % held_blk, 1), :] - sum_squares(cells) / feat) * to_score,
    )

    def bias(tile, start, cells):
        return (spread(cp_ref, tile, blocks, tiles_blk) - sum_squares(cells) / feat) * to_score

    other_records(next_ref.at[near_side(True)], yrec, build, feat, tiles_blk, tiles, bias)
    ext_records(prog_ref.at[near_side(True)], ext, progs, tiles_blk, tiles)
    acc[...] = back_ref[...]
    width = TILE // SPLITS
    for owner in range(blocks):
        for place in range(held_blk):
            start = lane_of(owner, place, blocks)
            rows_ref[:, start : start + width] = home_ref[owner, place : place + 1, :]
            cols_ref[:, start : start + width] = cp_ref[owner, lax.axis_index("blk"), place : place + 1, :]

    def use(scores_ref, top, row, col):
        plan = jnp.exp2(scores_ref[...]).astype(jnp.bfloat16)
        acc[row] = acc[row] + jnp.dot(ext[col], plan, preferred_element_type=jnp.float32)

    over_pairs(groups, ready, None, yrec, xrec, mine, other, use)
    for tile in range(held):
        sums = acc[tile]
        out_ref[tile // held_blk, tile % held_blk] = (sums[0:progs] / sums[progs : progs + 1]).astype(jnp.bfloat16)


MESH = pl.DeviceIdType.MESH


def greet(targets):
    barrier = pltpu.get_barrier_semaphore()
    expected = jnp.int32(0)
    for used, sec, blk in targets:

        @pl.when(used)
        def _():
            pl.semaphore_signal(barrier, inc=1, device_id=(sec, blk), device_id_type=MESH)

        expected = expected + jnp.where(used, 1, 0)
    pl.semaphore_wait(barrier, expected)


def send(src, dst, sems, place, sec, blk):
    return pltpu.make_async_remote_copy(
        src_ref=src, dst_ref=dst, send_sem=sems[0].at[place], recv_sem=sems[1].at[place],
        device_id=(sec, blk), device_id_type=MESH,
    )


STAGES = 8


def gather_kernel(counts, x_ref, prog_ref, pot_ref, list_ref, own_ref, xs_ref, progs_ref, pots_ref, lists_ref,
                  all_lists_ref, send_sem, recv_sem, mate_send, mate_recv):
    n_sec, blocks = counts
    sec, blk = lax.axis_index("sec"), lax.axis_index("blk")
    even = sec % 2 == 0
    partner = jnp.where(even, sec + 1, sec - 1)
    relay_to = jnp.where(even, sec + 2, sec - 2)
    relay_from = jnp.where(even, sec - 2, sec + 2)
    has_to = jnp.logical_and(relay_to >= 0, relay_to < n_sec)
    has_from = jnp.logical_and(relay_from >= 0, relay_from < n_sec)
    core = blk + 1 - 2 * (blk % 2)
    across = (blk + 2) % blocks
    corner = core + 2 - 4 * (core // 2)
    mates = (core, across, corner)
    yes = sec >= 0
    greet(
        [(yes, partner, blk), (has_to, relay_to, blk), (has_from, relay_from, blk)]
        + [(yes, sec, mate) for mate in mates]
    )
    sems, mate_sems = (send_sem, recv_sem), (mate_send, mate_recv)
    width = TILE // SPLITS
    held_blk = x_ref.shape[1] // TILE * SPLITS // blocks
    half = x_ref.shape[1] // 2
    sources = [
        (list_ref, lists_ref, None), (x_ref, xs_ref, 0), (x_ref, xs_ref, 1), (prog_ref, progs_ref, 0), (prog_ref, progs_ref, 1),
    ]

    def cut(ref, part):
        return ref if part is None else ref.at[:, part * half : (part + 1) * half]

    def place_of(buffer, side, owner, part):
        return cut(buffer.at[side, owner], part)

    def first(c):
        src, buffer, part = sources[c]
        return send(cut(src, part), place_of(buffer, 0, blk, part), sems, STAGES * c, partner, blk)

    def relay(c):
        _, buffer, part = sources[c]
        return send(
            place_of(buffer, 0, blk, part), place_of(buffer, 1, blk, part), sems, STAGES * c + 1, relay_to, blk
        )

    def share(c, side, kind):
        _, buffer, part = sources[c]
        owner = across if kind == 2 else blk
        slot = place_of(buffer, side, owner, part)
        return send(slot, slot, sems, STAGES * c + 2 + 3 * side + kind, sec, across if kind == 0 else core)

    def to_mate(k):
        mate = mates[k]
        copies = []
        for tile in range(held_blk):
            start = pl.multiple_of(lane_of(mate, tile, blocks), width)
            copies.append((x_ref.at[:, pl.ds(start, width)], own_ref.at[blk, tile]))
        copies.append((pot_ref, pots_ref.at[blk]))
        copies.append((list_ref, all_lists_ref.at[blk]))
        per = len(copies)
        return [send(src, dst, mate_sems, per * k + n, sec, mate) for n, (src, dst) in enumerate(copies)]

    chunks = range(len(sources))
    for c in chunks:
        first(c).start()
    for k in range(3):
        for copy in to_mate(k):
            copy.start()
    for tile in range(held_blk):
        start = pl.multiple_of(lane_of(blk, tile, blocks), width)
        own_ref[blk, tile] = x_ref[:, pl.ds(start, width)]
    pots_ref[blk] = pot_ref[...]
    all_lists_ref[blk] = list_ref[...]
    for turn in range(len(sources) + 2):
        if turn in chunks:
            first(turn).wait_recv()

            @pl.when(has_to)
            def _():
                relay(turn).start()

            share(turn, 0, 0).start()
            share(turn, 0, 1).start()
        if turn - 1 in chunks:
            share(turn - 1, 0, 0).wait_recv()
            share(turn - 1, 0, 2).start()

            @pl.when(has_from)
            def _():
                relay(turn - 1).wait_recv()
                share(turn - 1, 1, 0).start()
                share(turn - 1, 1, 1).start()

        if turn - 2 in chunks:

            @pl.when(has_from)
            def _():
                share(turn - 2, 1, 0).wait_recv()
                share(turn - 2, 1, 2).start()

    for c in chunks:
        for kind in (1, 2):
            share(c, 0, kind).wait_recv()

    @pl.when(has_from)
    def _():
        for c in chunks:
            for kind in (1, 2):
                share(c, 1, kind).wait_recv()

    for k in range(3):
        for copy in to_mate(k):
            copy.wait_recv()
    for c in chunks:
        first(c).wait_send()
        for kind in range(3):
            share(c, 0, kind).wait_send()

    @pl.when(has_to)
    def _():
        for c in chunks:
            relay(c).wait_send()

    @pl.when(has_from)
    def _():
        for c in chunks:
            for kind in range(3):
                share(c, 1, kind).wait_send()

    for k in range(3):
        for copy in to_mate(k):
            copy.wait_send()


def shift_kernel(counts, steps, home, part_ref, out_ref, *rest):
    home_ref = rest[0] if home else None
    send_sem, recv_sem = rest[-2:]
    n_sec, blocks = counts
    sec, blk = lax.axis_index("sec"), lax.axis_index("blk")
    to, source = sec + steps, sec - steps
    has_to = jnp.logical_and(to >= 0, to < n_sec)
    has_from = jnp.logical_and(source >= 0, source < n_sec)
    targets = [(blk + turn) % blocks for turn in range(blocks)]
    mates = [(sec >= 0, sec, mate) for mate in targets[1:]] if home else []
    greet(mates + [(has_to, to, mate) for mate in targets] + [(has_from, source, mate) for mate in targets])

    def copy(turn):
        return send(part_ref, out_ref.at[blk], (send_sem, recv_sem), turn, to, targets[turn])

    def homeward(turn, owner):
        src = part_ref.at[targets[turn]]
        return send(src, home_ref.at[owner], (send_sem, recv_sem), blocks + turn - 1, sec, targets[turn])

    def arrival(turn):
        slot = out_ref.at[(blk + blocks - turn) % blocks]
        return send(part_ref, slot, (send_sem, recv_sem), turn, to, targets[turn])

    @pl.when(has_to)
    def _():
        for turn in range(blocks):
            copy(turn).start()

    if home:
        for turn in range(1, blocks):
            homeward(turn, blk).start()
        home_ref[blk] = part_ref[blk]
        for turn in range(1, blocks):
            homeward(turn, (blk + blocks - turn) % blocks).wait_recv()

    @pl.when(has_from)
    def _():
        for turn in range(blocks):
            arrival(turn).wait_recv()

    @pl.when(jnp.logical_not(has_from))
    def _():
        out_ref[...] = jnp.zeros_like(out_ref)

    @pl.when(has_to)
    def _():
        for turn in range(blocks):
            copy(turn).wait_send()

    if home:
        for turn in range(1, blocks):
            homeward(turn, blk).wait_send()


def return_kernel(counts, smooth_ref, out_ref, send_sem, recv_sem):
    n_sec, blocks = counts
    sec, blk = lax.axis_index("sec"), lax.axis_index("blk")
    held_blk, width = smooth_ref.shape[1], smooth_ref.shape[3]
    mates = [(blk + turn) % blocks for turn in range(blocks)]
    greet([(sec >= 0, sec, mate) for mate in mates[1:]])

    def copies(turn, owner):
        found = []
        for place in range(held_blk):
            start = pl.multiple_of(lane_of(owner, place, blocks), width)
            src, dst = smooth_ref.at[mates[turn], place], out_ref.at[:, pl.ds(start, width)]
            found.append(send(src, dst, (send_sem, recv_sem), held_blk * (turn - 1) + place, sec, mates[turn]))
        return found

    for turn in range(1, blocks):
        for copy in copies(turn, blk):
            copy.start()
    for place in range(held_blk):
        start = pl.multiple_of(lane_of(blk, place, blocks), width)
        out_ref[:, pl.ds(start, width)] = smooth_ref[blk, place]
    for turn in range(1, blocks):
        for copy in copies(turn, (blk + blocks - turn) % blocks):
            copy.wait_recv()
    for turn in range(1, blocks):
        for copy in copies(turn, blk):
            copy.wait_send()


def in_vmem(count):
    return [pl.BlockSpec(memory_space=pltpu.VMEM)] * count


def exchange(kernel, number, out_shape, operands, scratch):
    outs = jax.tree.map(lambda _: pl.BlockSpec(memory_space=pltpu.VMEM), out_shape)
    return pl.pallas_call(
        kernel, out_shape=out_shape, in_specs=in_vmem(len(operands)), out_specs=outs, scratch_shapes=scratch,
        compiler_params=pltpu.CompilerParams(collective_id=number, has_side_effects=True),
    )(*operands)


def call(kernel, out_shape, operands, scratch):
    outs = jax.tree.map(lambda _: pl.BlockSpec(memory_space=pltpu.VMEM), out_shape)
    return pl.pallas_call(
        kernel, out_shape=out_shape,
        in_specs=[pl.BlockSpec(memory_space=pltpu.SMEM)] + in_vmem(len(operands) - 1),
        out_specs=outs, scratch_shapes=scratch,
    )(*operands)


def body(features, programs, column_pot, tile_pairs, pair_counts):
    feat, cells_blk = features.shape[1:]
    progs = programs.shape[1]
    tiles_blk = cells_blk // TILE
    most = tile_pairs.shape[2]
    blocks, n_sec = lax.axis_size("blk"), lax.axis_size("sec")
    tiles = tiles_blk * blocks
    width = TILE // SPLITS
    held_blk = tiles_blk * SPLITS // blocks
    held = blocks * held_blk
    dims = (feat, blocks, tiles_blk, most)
    counts = (n_sec, blocks)
    f32, bf16 = jnp.float32, jnp.bfloat16
    shape = jax.ShapeDtypeStruct
    long = -(-(2 * most + 1) // 128) * 128
    listed = jnp.concatenate([tile_pairs[0], tile_pairs[1], pair_counts], axis=1)
    listed = jnp.pad(listed, ((0, 0), (0, long - listed.shape[1])))
    dma = pltpu.SemaphoreType.DMA
    mate_copies = (blocks - 1) * (held_blk + 2)

    own, xs, progs_all, pot, lists_all, lists = exchange(
        functools.partial(gather_kernel, counts), 0,
        (
            shape((blocks, held_blk, feat, width), bf16),
            shape((2, blocks, feat, cells_blk), bf16),
            shape((2, blocks, progs, cells_blk), bf16),
            shape((blocks, 1, cells_blk), bf16),
            shape((2, blocks, 1, long), jnp.int32),
            shape((blocks, 1, long), jnp.int32),
        ),
        (features[0], programs[0], column_pot, listed),
        [dma((STAGES * 5,)), dma((STAGES * 5,)), dma((mate_copies,)), dma((mate_copies,))],
    )

    xrec = pltpu.VMEM((held, 2 * HALF, width), bf16)
    yrec = pltpu.VMEM(((tiles + 1) * TILE, 2 * HALF), bf16)
    build = pltpu.VMEM((tiles_blk, 2 * HALF, TILE), f32)
    ext = pltpu.VMEM((tiles + 1, EXT, TILE), bf16)
    stat = pltpu.VMEM((held, 1, width), f32)
    acc = pltpu.VMEM((held, EXT, width), f32)
    index = pltpu.SMEM((blocks * most + 2 * UNROLL,), jnp.int32)
    ready = [pltpu.VMEM((TILE, width), f32)] * UNROLL
    tops = pltpu.VMEM((UNROLL, 1, width), f32)
    pots = shape((blocks, held_blk, width), f32)
    all_pots = shape((blocks, blocks, held_blk, width), f32)
    sums = shape((held, EXT, width), f32)

    row_own = call(
        functools.partial(row_kernel, dims), pots, (lists, own, xs, pot),
        [xrec, yrec, build, stat, stat, index, index, *ready],
    )
    row_prev, row_home = exchange(
        functools.partial(shift_kernel, counts, 1, True), 1, (all_pots, pots), (row_own,),
        [dma((2 * blocks - 1,)), dma((2 * blocks - 1,))],
    )
    col_own, back = call(
        functools.partial(col_kernel, dims), (pots, sums), (lists_all, own, xs, row_prev, progs_all),
        [xrec, yrec, build, ext, stat, stat, acc, index, index, tops, *ready],
    )
    col_all = exchange(
        functools.partial(shift_kernel, counts, -1, False), 2, all_pots, (col_own,), [dma((blocks,)), dma((blocks,))]
    )
    line = shape((1, cells_blk), f32)
    smooth, row_out, col_out = call(
        functools.partial(plan_kernel, dims),
        (shape((blocks, held_blk, progs, width), bf16), line, line),
        (lists, own, xs, row_own, col_all, progs_all, back, row_home),
        [xrec, yrec, build, ext, acc, index, index, *ready],
    )
    return_copies = (blocks - 1) * held_blk
    smoothed = exchange(
        functools.partial(return_kernel, counts), 3, shape((progs, cells_blk), bf16), (smooth,),
        [dma((return_copies,)), dma((return_copies,))],
    )
    return smoothed[None], row_out, col_out


def solution(mesh):
    in_specs = (
        P("sec", None, "blk"),
        P("sec", None, "blk"),
        P("sec", "blk"),
        P(None, "sec", "blk"),
        P("sec", "blk"),
    )
    out_specs = (P("sec", None, "blk"), P("sec", "blk"), P("sec", "blk"))
    return jax.shard_map(body, mesh=mesh, in_specs=in_specs, out_specs=out_specs, check_vma=False)
```
